32 devices in a mesh: dp: 2 (over x), fsdp: 16 (over z, y, core).
Axes of the slice: x: 2, y: 2, z: 4, core: 2. Of those that a mesh axis runs over, the one named last changes fastest.
Arguments:
- tokens: bfloat16 [16384, 1024], P(('dp', 'fsdp')), may hold values from -6 to 6
- doc_ids: int32 [16384], P(('dp', 'fsdp')), may hold values from 0 to 3, as said below
- live_mask: int32 [16384], P(('dp', 'fsdp')), may hold values from 0 to 1, as said below
- w_query: bfloat16 [2, 1024, 1024], P(None, ('dp', 'fsdp')), may hold values from -0.1875 to 0.1875
- w_key: bfloat16 [2, 1024, 1024], P(None, ('dp', 'fsdp')), may hold values from -0.1875 to 0.1875
- w_value: bfloat16 [2, 1024, 1024], P(None, ('dp', 'fsdp')), may hold values from -0.1875 to 0.1875
- w_out: bfloat16 [2, 1024, 1024], P(None, ('dp', 'fsdp')), may hold values from -0.75 to 0.75
- w_gate: bfloat16 [2, 1024, 2816], P(None, ('dp', 'fsdp')), may hold values from -0.1875 to 0.1875
- w_up: bfloat16 [2, 1024, 2816], P(None, ('dp', 'fsdp')), may hold values from -0.1875 to 0.1875
- w_down: bfloat16 [2, 2816, 1024], P(None, ('dp', 'fsdp')), may hold values from -0.109375 to 0.109375
- gain_attn: bfloat16 [2, 1024], P(None, ('dp', 'fsdp')), may hold values from 0.5 to 1.5
- gain_ffn: bfloat16 [2, 1024], P(None, ('dp', 'fsdp')), may hold values from 0.5 to 1.5
- cotangent: bfloat16 [16384, 1024], P(('dp', 'fsdp')), may hold values from -6 to 6
Outputs:
- output: bfloat16 [16384, 1024], P(('dp', 'fsdp'))
- grad_tokens: bfloat16 [16384, 1024], P(('dp', 'fsdp'))
- grad_w_query: float32 [2, 1024, 1024], P(None, ('dp', 'fsdp'))
- grad_w_key: float32 [2, 1024, 1024], P(None, ('dp', 'fsdp'))
- grad_w_value: float32 [2, 1024, 1024], P(None, ('dp', 'fsdp'))
- grad_w_out: float32 [2, 1024, 1024], P(None, ('dp', 'fsdp'))
- grad_w_gate: float32 [2, 1024, 2816], P(None, ('dp', 'fsdp'))
- grad_w_up: float32 [2, 1024, 2816], P(None, ('dp', 'fsdp'))
- grad_w_down: float32 [2, 2816, 1024], P(None, ('dp', 'fsdp'))
- grad_gain_attn: float32 [2, 1024], P(None, ('dp', 'fsdp'))
- grad_gain_ffn: float32 [2, 1024], P(None, ('dp', 'fsdp'))
The draws below stay inside these ranges and needn't reach their ends.
Inputs may be any that keep to these rules, and one draw needn't show every extreme that they name: `doc_ids`: sequence number of a slot within its aligned bucket of 512 slots (the slots of one device); it never falls within a bucket, so each sequence is a run of slots, and numbering starts afresh in every bucket; some bucket holds a single sequence over all its slots. `live_mask`: 1 on the first slots of every aligned bucket of 512 and 0 on the rest; at least half of every bucket is live, and some bucket is live throughout.
All inputs are finite; a program needn't handle non-finite values.
Results may differ from the reference program's by a relative error of at most 0.02.
Values may be sent and summed in bfloat16 or wider, within the bound.
A program may use at most 320 MiB of HBM per device.

```python
import jax
import jax.numpy as jnp
from jax import lax

D = 1024
H = 16
HD = 64
FF = 2816
TOK_DEV = 512
TOKENS = 16384


def sequence_draw(key):
    block_count = TOKENS // TOK_DEV
    keys_all = jax.random.split(jax.random.fold_in(key, 11), 4)
    padding = jax.random.randint(keys_all[0], (block_count,), 0, TOK_DEV // 2 + 1)
    full_block = jax.random.randint(keys_all[1], (), 0, block_count)
    block_index = jnp.arange(block_count)
    is_full = block_index == full_block
    is_split = block_index == (full_block + 1) % block_count
    padding = jnp.where(is_full, 0, jnp.where(is_split, TOK_DEV // 2, padding))
    cut_rows = jax.random.randint(keys_all[2], (block_count, 3), 1, TOK_DEV)
    cut_used = jax.random.randint(keys_all[3], (block_count, 3), 0, 5) < 3
    cut_used = (cut_used | is_split[:, None]) & jnp.logical_not(is_full)[:, None]
    row_index = jnp.arange(TOK_DEV)
    crossed = cut_used[:, :, None] & (cut_rows[:, :, None] <= row_index[None, None, :])
    doc_ids = jnp.sum(crossed.astype(jnp.int32), axis=1)
    live_mask = (row_index[None, :] < TOK_DEV - padding[:, None]).astype(jnp.int32)
    return (doc_ids.reshape(-1), live_mask.reshape(-1))


def draw_doc_ids(key, part):
    return sequence_draw(key)[0]


def draw_live_mask(key, part):
    return sequence_draw(key)[1]


def levels(stream_key, extent, pieces, low, top_value):
    def one(dim, blocks):
        draws = jax.random.uniform(jax.random.fold_in(jax.random.fold_in(stream_key, 6), dim), (blocks,), jnp.float32, low / len(pieces), top_value / len(pieces))
        return jnp.repeat(jnp.exp(draws), extent[dim] // blocks).reshape((-1,) + (1,) * (len(extent) - dim - 1))

    gain = one(*pieces[0])
    for cut in pieces[1:]:
        gain = gain * one(*cut)
    return gain


def bell_draw(own_key, extent, scale, bound, shards=(), kind=jnp.bfloat16):
    entries = scale * jax.random.normal(own_key, extent, jnp.float32)
    if shards:
        entries = entries * levels(own_key, extent, shards, -0.22, 0.18)
    return jnp.clip(entries, -bound, bound).astype(kind)


def setup_inputs(seed: int = 0) -> dict:
    arg_keys = jax.random.split(jax.random.key(seed), 14)
    return {
        "tokens": bell_draw(arg_keys[0], (TOKENS, D), 1.0, 6.0, ((0, 32),)),
        "doc_ids": draw_doc_ids(jax.random.fold_in(arg_keys[13], 71), 0),
        "live_mask": draw_live_mask(jax.random.fold_in(arg_keys[13], 71), 0),
        "w_query": bell_draw(arg_keys[3], (2, D, D), D ** -0.5, 0.1875, ((1, 32),)),
        "w_key": bell_draw(arg_keys[4], (2, D, D), D ** -0.5, 0.1875, ((1, 32),)),
        "w_value": bell_draw(arg_keys[5], (2, D, D), D ** -0.5, 0.1875, ((1, 32),)),
        "w_out": bell_draw(arg_keys[6], (2, D, D), (D // 16) ** -0.5, 0.75, ((1, 32),)),
        "w_gate": bell_draw(arg_keys[7], (2, D, FF), D ** -0.5, 0.1875, ((1, 32),)),
        "w_up": bell_draw(arg_keys[8], (2, D, FF), D ** -0.5, 0.1875, ((1, 32),)),
        "w_down": bell_draw(arg_keys[9], (2, FF, D), FF ** -0.5, 0.109375, ((1, 32),)),
        "gain_attn": jnp.clip(1.0 + 0.1 * jax.random.normal(arg_keys[10], (2, D), jnp.float32), 0.5, 1.5).astype(jnp.bfloat16),
        "gain_ffn": jnp.clip(1.0 + 0.1 * jax.random.normal(arg_keys[11], (2, D), jnp.float32), 0.5, 1.5).astype(jnp.bfloat16),
        "cotangent": bell_draw(arg_keys[12], (TOKENS, D), 1.0, 6.0, ((0, 32),)),
    }


@jax.custom_vjp
def low(v):
    return lax.optimization_barrier(v.astype(jnp.bfloat16)).astype(jnp.float32)

@jax.custom_vjp
def low_back(v):
    return v

def low_keep(v):
    return (low(v), None)

def low_pass(kept, grad):
    return (grad,)

def back_keep(v):
    return (v, None)

def back_low(kept, grad):
    return (low(grad),)
low.defvjp(low_keep, low_pass)
low_back.defvjp(back_keep, back_low)
EPSILON = 1e-06
ROPE_BASE = 10000.0
MASKED = -1000000000.0
PRECISE = lax.Precision.HIGHEST

def matmul(left, right):
    return jnp.dot(left, right, precision=PRECISE, preferred_element_type=jnp.float32)

def positions(doc_ids):
    buckets = doc_ids.reshape(-1, TOK_DEV)
    earlier = lax.optimization_barrier(jnp.sum((buckets[:, None, :] < buckets[:, :, None]).astype(jnp.int32), axis=2))
    return (jnp.arange(TOK_DEV, dtype=jnp.int32)[None, :] - earlier).reshape(-1)

def rope_tables(position):
    freq_table = ROPE_BASE ** (-jnp.arange(HD // 2, dtype=jnp.float32) * 2.0 / HD)
    angles = position.astype(jnp.float32)[:, None] * freq_table[None, :]
    return (jnp.cos(angles), jnp.sin(angles))

def rotate(matrix, cosine, sine_table, direction):
    row_count = matrix.shape[0]
    heads = matrix.reshape(row_count, H, HD)
    first_half = heads[..., :HD // 2]
    second_half = heads[..., HD // 2:]
    cos_part = cosine[:, None, :]
    sin_part = direction * sine_table[:, None, :]
    turned = jnp.concatenate([first_half * cos_part - second_half * sin_part, second_half * cos_part + first_half * sin_part], axis=-1)
    return turned.reshape(row_count, H * HD)

def normalize(hidden, gain_row):
    inverse_rms = lax.rsqrt(lax.optimization_barrier(jnp.mean(hidden * hidden, axis=1, keepdims=True)) + EPSILON)
    return hidden * inverse_rms * gain_row[None, :]

def attend_block(packed):
    query_rot, key_rot, mixed, doc_block, live_block = packed
    row_count = query_rot.shape[0]
    query_heads = query_rot.reshape(row_count, H, HD)
    key_heads = key_rot.reshape(row_count, H, HD)
    value_heads = mixed.reshape(row_count, H, HD)
    scores = jnp.einsum('qhd,khd->hqk', query_heads, key_heads, precision=PRECISE) * HD ** (-0.5)
    scores = low_back(scores)
    row_index = jnp.arange(row_count)
    allowed = (row_index[None, :] == row_index[:, None]) | (row_index[None, :] < row_index[:, None]) & (doc_block[None, :] == doc_block[:, None]) & (live_block[None, :] > 0)
    scores = jnp.where(allowed[None], scores, MASKED)
    row_max = lax.optimization_barrier(jnp.max(scores, axis=2, keepdims=True))
    weights = jnp.exp(scores - row_max)
    attn_prob = low(weights / lax.optimization_barrier(jnp.sum(weights, axis=2, keepdims=True)))
    context = jnp.einsum('hqk,khd->qhd', attn_prob, value_heads, precision=PRECISE)
    return context.reshape(row_count, H * HD)

def attend(query_rot, key_rot, mixed, doc_ids, live_mask):

    def blocks(matrix):
        return matrix.reshape(-1, TOK_DEV, matrix.shape[-1])
    context = lax.map(jax.checkpoint(attend_block), (blocks(query_rot), blocks(key_rot), blocks(mixed), doc_ids.reshape(-1, TOK_DEV), live_mask.reshape(-1, TOK_DEV)))
    return context.reshape(-1, H * HD)

def decoder_layer(hidden, params, values_first, doc_ids, live_mask, cosine, sine_table):
    query_weight, key_weight, value_weight, out_weight, gate_weight, up_weight, down_weight, attn_gain, ffn_gain = params
    normed_one = low(normalize(hidden, attn_gain))
    query = low_back(matmul(normed_one, query_weight))
    key_rows = low_back(matmul(normed_one, key_weight))
    values = low_back(matmul(normed_one, value_weight))
    if values_first is None:
        mixed = values
    else:
        mixed = 0.5 * values + 0.5 * values_first
    query_rot = low(rotate(query, cosine, sine_table, 1.0))
    key_rot = low(rotate(key_rows, cosine, sine_table, 1.0))
    context = low_back(attend(query_rot, key_rot, low(mixed), doc_ids, live_mask))
    middle = hidden + low_back(matmul(low(context), out_weight))
    normed_two = low(normalize(middle, ffn_gain))
    gate = low_back(matmul(normed_two, gate_weight))
    up_part = low_back(matmul(normed_two, up_weight))
    hidden_ffn = low(jax.nn.silu(gate) * up_part)
    result = middle + low_back(matmul(hidden_ffn, down_weight))
    return (result, values)

def forward(token_rows, weights, doc_ids, live_mask, cosine, sine_table):
    layer_one = tuple((matrix[0] for matrix in weights))
    layer_two = tuple((matrix[1] for matrix in weights))
    middle_rows, values_first = decoder_layer(token_rows, layer_one, None, doc_ids, live_mask, cosine, sine_table)
    result, unused = decoder_layer(middle_rows, layer_two, values_first, doc_ids, live_mask, cosine, sine_table)
    return result * live_mask.astype(jnp.float32)[:, None]

def reference(tokens, doc_ids, live_mask, w_query, w_key, w_value, w_out, w_gate, w_up, w_down, gain_attn, gain_ffn, cotangent):
    cosine, sine_table = rope_tables(positions(doc_ids))
    weights = tuple((matrix.astype(jnp.float32) for matrix in (w_query, w_key, w_value, w_out, w_gate, w_up, w_down, gain_attn, gain_ffn)))

    def run_forward(token_rows, params):
        return forward(token_rows, params, doc_ids, live_mask, cosine, sine_table)
    result, pullback = jax.vjp(run_forward, tokens.astype(jnp.float32), weights)
    grad_tokens, grads = pullback(cotangent.astype(jnp.float32))
    return (result.astype(jnp.bfloat16), grad_tokens.astype(jnp.bfloat16), grads[0], grads[1], grads[2], grads[3], grads[4], grads[5], grads[6], grads[7], grads[8])
```

```python
import functools

import jax
import jax.numpy as jnp
from jax import lax
from jax.experimental import pallas as pl
from jax.experimental.pallas import tpu as pltpu
from jax.sharding import PartitionSpec as P

H = 16
HD = 64


EPSILON = 1e-06
ROPE_BASE = 10000.0
MASKED = -1000000000.0


def matmul(left, right):
    return jnp.dot(left, right, preferred_element_type=jnp.float32)


def inner_rows(left, right):
    return lax.dot_general(
        left, right, (((0,), (0,)), ((), ())), preferred_element_type=jnp.float32
    )


def times_transposed(left, right):
    return lax.dot_general(
        left, right, (((1,), (1,)), ((), ())), preferred_element_type=jnp.float32
    )


def sequence_layout(doc_ids, live_mask):
    row_count = doc_ids.shape[0]
    earlier = jnp.sum((doc_ids[None, :] < doc_ids[:, None]).astype(jnp.int32), axis=1)
    row_index = jnp.arange(row_count, dtype=jnp.int32)
    position = row_index - earlier
    allowed = (row_index[None, :] == row_index[:, None]) | (
        row_index[None, :] < row_index[:, None]
    ) & (doc_ids[None, :] == doc_ids[:, None]) & (live_mask[None, :] > 0)
    return (position, allowed)


def rope_tables(position):
    freq_table = ROPE_BASE ** (-jnp.arange(HD // 2, dtype=jnp.float32) * 2.0 / HD)
    angles = position.astype(jnp.float32)[:, None] * freq_table[None, :]
    return (jnp.cos(angles), jnp.sin(angles))


def rotate(matrix, cosine, sine_table, direction):
    row_count = matrix.shape[0]
    heads = matrix.reshape(row_count, H, HD)
    first_half = heads[..., : HD // 2]
    second_half = heads[..., HD // 2 :]
    cos_part = cosine[:, None, :]
    sin_part = direction * sine_table[:, None, :]
    turned = jnp.concatenate(
        [
            first_half * cos_part - second_half * sin_part,
            second_half * cos_part + first_half * sin_part,
        ],
        axis=-1,
    )
    return turned.reshape(row_count, H * HD)


def rms_scale(hidden):
    return lax.rsqrt(jnp.mean(hidden * hidden, axis=1, keepdims=True) + EPSILON)


def norm_backward(grad_normed, unit_rows, inverse_rms, gain_row):
    grad_gain = jnp.sum(grad_normed * unit_rows, axis=0)
    grad_unit = grad_normed * gain_row.astype(jnp.float32)[None, :]
    grad_input = inverse_rms * (
        grad_unit - unit_rows * jnp.mean(grad_unit * unit_rows, axis=1, keepdims=True)
    )
    return (grad_gain, grad_input)


def attention_forward(query_rot, key_rot, mixed_low, allowed):
    row_count = query_rot.shape[0]
    query_heads = query_rot.reshape(row_count, H, HD)
    key_heads = key_rot.reshape(row_count, H, HD)
    value_heads = mixed_low.reshape(row_count, H, HD)
    scores = jnp.einsum(
        "qhd,khd->hqk", query_heads, key_heads, preferred_element_type=jnp.float32
    ) * HD ** (-0.5)
    scores = jnp.where(allowed[None], scores, MASKED)
    row_max = jnp.max(scores, axis=2, keepdims=True)
    weights = jnp.exp(scores - row_max)
    total = jnp.sum(weights, axis=2, keepdims=True)
    prob_low = (weights / total).astype(jnp.bfloat16)
    context = jnp.einsum("hqk,khd->qhd", prob_low, value_heads, preferred_element_type=jnp.float32)
    return (context.reshape(row_count, H * HD), row_max + jnp.log(total))


def attention_backward(query_rot, key_rot, mixed_low, log_norm, allowed, grad_context):
    row_count = query_rot.shape[0]
    query_heads = query_rot.reshape(row_count, H, HD)
    key_heads = key_rot.reshape(row_count, H, HD)
    value_heads = mixed_low.reshape(row_count, H, HD)
    grad_heads = grad_context.reshape(row_count, H, HD)
    scores = jnp.einsum(
        "qhd,khd->hqk", query_heads, key_heads, preferred_element_type=jnp.float32
    ) * HD ** (-0.5)
    attn_prob = jnp.where(allowed[None], jnp.exp(scores - log_norm), 0.0)
    prob_low = attn_prob.astype(jnp.bfloat16)
    grad_mixed = jnp.einsum(
        "hqk,qhd->khd", prob_low, grad_heads, preferred_element_type=jnp.float32
    )
    grad_prob = jnp.einsum(
        "qhd,khd->hqk", grad_heads, value_heads, preferred_element_type=jnp.float32
    )
    row_inner = jnp.sum(attn_prob * grad_prob, axis=2, keepdims=True)
    grad_scores = (attn_prob * (grad_prob - row_inner)).astype(jnp.bfloat16)
    grad_query_rot = jnp.einsum(
        "hqk,khd->qhd", grad_scores, key_heads, preferred_element_type=jnp.float32
    ) * HD ** (-0.5)
    grad_key_rot = jnp.einsum(
        "hqk,qhd->khd", grad_scores, query_heads, preferred_element_type=jnp.float32
    ) * HD ** (-0.5)
    return (
        grad_query_rot.reshape(row_count, H * HD),
        grad_key_rot.reshape(row_count, H * HD),
        grad_mixed.reshape(row_count, H * HD),
    )


def layer_forward(hidden, params, values_first, allowed, cosine, sine_table):
    (
        query_weight,
        key_weight,
        value_weight,
        out_weight,
        gate_weight,
        up_weight,
        down_weight,
        attn_gain,
        ffn_gain,
    ) = params
    inverse_one = rms_scale(hidden)
    unit_one = hidden * inverse_one
    normed_one = (unit_one * attn_gain.astype(jnp.float32)[None, :]).astype(jnp.bfloat16)
    query = matmul(normed_one, query_weight)
    key_rows = matmul(normed_one, key_weight)
    values = matmul(normed_one, value_weight)
    if values_first is None:
        mixed = values
    else:
        mixed = 0.5 * values + 0.5 * values_first
    mixed_low = mixed.astype(jnp.bfloat16)
    query_rot = rotate(query, cosine, sine_table, 1.0).astype(jnp.bfloat16)
    key_rot = rotate(key_rows, cosine, sine_table, 1.0).astype(jnp.bfloat16)
    context, log_norm = attention_forward(query_rot, key_rot, mixed_low, allowed)
    context_low = context.astype(jnp.bfloat16)
    middle = hidden + matmul(context_low, out_weight)
    inverse_two = rms_scale(middle)
    unit_two = middle * inverse_two
    normed_two = (unit_two * ffn_gain.astype(jnp.float32)[None, :]).astype(jnp.bfloat16)
    gate = matmul(normed_two, gate_weight)
    up_part = matmul(normed_two, up_weight)
    hidden_ffn = (jax.nn.silu(gate) * up_part).astype(jnp.bfloat16)
    result = middle + matmul(hidden_ffn, down_weight)
    saved = (
        inverse_one,
        unit_one,
        normed_one,
        mixed_low,
        query_rot,
        key_rot,
        log_norm,
        context_low,
        inverse_two,
        unit_two,
        normed_two,
        gate,
        up_part,
        hidden_ffn,
    )
    return (result, values, saved)


def layer_backward(grad_result, params, saved, carried_in, is_later, allowed, cosine, sine_table):
    (
        query_weight,
        key_weight,
        value_weight,
        out_weight,
        gate_weight,
        up_weight,
        down_weight,
        attn_gain,
        ffn_gain,
    ) = params
    (
        inverse_one,
        unit_one,
        normed_one,
        mixed_low,
        query_rot,
        key_rot,
        log_norm,
        context_low,
        inverse_two,
        unit_two,
        normed_two,
        gate,
        up_part,
        hidden_ffn,
    ) = saved
    grad_down_in = grad_result.astype(jnp.bfloat16)
    grad_w_down = inner_rows(hidden_ffn, grad_down_in)
    grad_ffn_hidden = times_transposed(grad_down_in, down_weight)
    sigma = jax.nn.sigmoid(gate)
    grad_gate = (grad_ffn_hidden * up_part * sigma * (1.0 + gate * (1.0 - sigma))).astype(
        jnp.bfloat16
    )
    grad_up = (grad_ffn_hidden * gate * sigma).astype(jnp.bfloat16)
    grad_w_gate = inner_rows(normed_two, grad_gate)
    grad_w_up = inner_rows(normed_two, grad_up)
    grad_normed_two = times_transposed(grad_gate, gate_weight) + times_transposed(
        grad_up, up_weight
    )
    grad_gain_ffn, grad_from_norm = norm_backward(grad_normed_two, unit_two, inverse_two, ffn_gain)
    grad_middle = grad_result + grad_from_norm
    grad_branch = grad_middle.astype(jnp.bfloat16)
    grad_w_out = inner_rows(context_low, grad_branch)
    grad_context = times_transposed(grad_branch, out_weight).astype(jnp.bfloat16)
    grad_query_rot, grad_key_rot, grad_mixed = attention_backward(
        query_rot, key_rot, mixed_low, log_norm, allowed, grad_context
    )
    grad_query = rotate(grad_query_rot, cosine, sine_table, -1.0).astype(jnp.bfloat16)
    grad_key = rotate(grad_key_rot, cosine, sine_table, -1.0).astype(jnp.bfloat16)
    if is_later:
        grad_values = (0.5 * grad_mixed).astype(jnp.bfloat16)
        carried = 0.5 * grad_mixed
    else:
        grad_values = (grad_mixed + carried_in).astype(jnp.bfloat16)
        carried = None
    grad_w_query = inner_rows(normed_one, grad_query)
    grad_w_key = inner_rows(normed_one, grad_key)
    grad_w_value = inner_rows(normed_one, grad_values)
    grad_normed_one = (
        times_transposed(grad_query, query_weight)
        + times_transposed(grad_key, key_weight)
        + times_transposed(grad_values, value_weight)
    )
    grad_gain_attn, grad_from_first = norm_backward(
        grad_normed_one, unit_one, inverse_one, attn_gain
    )
    grad_hidden = grad_middle + grad_from_first
    grads = (
        grad_w_query,
        grad_w_key,
        grad_w_value,
        grad_w_out,
        grad_w_gate,
        grad_w_up,
        grad_w_down,
        grad_gain_attn,
        grad_gain_ffn,
    )
    return (grad_hidden, grads, carried)


MESH_ID = pl.DeviceIdType.MESH
VMEM_BYTES = 58 * 1024 * 1024


class Place:
    def __init__(self, z_count):
        self.z_count = z_count
        self.x = lax.axis_index("dp")
        f = lax.axis_index("fsdp")
        self.z = f // 4
        self.y = lax.rem(f, 4) // 2
        self.c = lax.rem(f, 2)

    def device(self, x, z, y, c):
        return (x, z * 4 + y * 2 + c)

    def x_mate(self):
        return self.device(1 - self.x, self.z, self.y, self.c)

    def y_mate(self):
        return self.device(self.x, self.z, 1 - self.y, self.c)

    def core_mate(self):
        return self.device(self.x, self.z, self.y, 1 - self.c)

    def z_plus(self, step):
        return lax.rem(self.z + step, self.z_count)

    def z_minus(self, step):
        return lax.rem(self.z + self.z_count - step, self.z_count)

    def z_mate(self, step):
        return self.device(self.x, self.z_plus(step), self.y, self.c)


def greet(place):
    barrier = pltpu.get_barrier_semaphore()
    mates = [place.x_mate(), place.y_mate(), place.core_mate()]
    mates += [place.z_mate(k) for k in range(1, place.z_count)]
    for mate in mates:
        pl.semaphore_signal(barrier, inc=1, device_id=mate, device_id_type=MESH_ID)
    pl.semaphore_wait(barrier, len(mates))


def remote(src, dst, send_sem, recv_sem, device):
    return pltpu.make_async_remote_copy(
        src_ref=src,
        dst_ref=dst,
        send_sem=send_sem,
        recv_sem=recv_sem,
        device_id=device,
        device_id_type=MESH_ID,
    )


def plan_pieces(widths):
    chunks = []
    for chunk in widths:
        chunks.append([(item, lo, hi, x_first) for item, lo, hi, x_first in chunk])
    return chunks


def gather_kernel(z_count, chunks, item_count, *refs):
    shards = refs[:item_count]
    outs = refs[item_count : 2 * item_count]
    local_sem, z_send, z_recv, hop_send, hop_recv = refs[2 * item_count :]
    place = Place(z_count)
    x, z, y, c = place.x, place.z, place.y, place.c
    every = slice(None)

    pieces = [piece for chunk in chunks for piece in chunk]
    number = {piece: index for index, piece in enumerate(pieces)}

    def window(piece, where):
        item, lo, hi, unused = piece
        return outs[item].at[tuple(where) + (every, pl.ds(lo, hi - lo))]

    def local_copy(piece):
        item, lo, hi, unused = piece
        return pltpu.make_async_copy(
            shards[item].at[:, pl.ds(lo, hi - lo)],
            window(piece, (x, z, y, c)),
            local_sem.at[number[piece]],
        )

    def z_copy(piece, step, arriving):
        item, lo, hi, unused = piece
        source_z = place.z_minus(step) if arriving else z
        return remote(
            shards[item].at[:, pl.ds(lo, hi - lo)],
            window(piece, (x, source_z, y, c)),
            z_send.at[number[piece], step - 1],
            z_recv.at[number[piece], step - 1],
            place.z_mate(step),
        )

    def hop(piece, stage, arriving):
        x_first = piece[3]
        if stage == 2:
            where = (every, every, every, 1 - c if arriving else c)
            mate = place.core_mate()
        elif (stage == 0) == x_first:
            along = (1 - x) if arriving else x
            where = (along, every, y if stage == 0 else every, c)
            mate = place.x_mate()
        else:
            along = (1 - y) if arriving else y
            where = (x if stage == 0 else every, every, along, c)
            mate = place.y_mate()
        ref = window(piece, where)
        return remote(
            ref, ref, hop_send.at[number[piece], stage], hop_recv.at[number[piece], stage], mate
        )

    greet(place)

    def start_z(chunk):
        for piece in chunk:
            local_copy(piece).start()
            for step in range(1, z_count):
                z_copy(piece, step, False).start()

    def finish_z(chunk):
        for piece in chunk:
            local_copy(piece).wait()
            for step in range(1, z_count):
                z_copy(piece, step, True).wait_recv()

    count = len(chunks)
    ahead = 3
    for t in range(min(ahead, count)):
        start_z(chunks[t])
    for t in range(count + 3):
        if t + ahead < count:
            start_z(chunks[t + ahead])
        if t < count:
            finish_z(chunks[t])
            for piece in chunks[t]:
                hop(piece, 0, False).start()
        for stage in (1, 2, 3):
            if 0 <= t - stage < count:
                for piece in chunks[t - stage]:
                    hop(piece, stage - 1, True).wait_recv()
                    if stage < 3:
                        hop(piece, stage, False).start()
    for piece in pieces:
        for step in range(1, z_count):
            z_copy(piece, step, False).wait_send()
        for stage in range(3):
            hop(piece, stage, False).wait_send()


def gather_weights(z_count, shards, chunks):
    pieces = sum(len(chunk) for chunk in chunks)
    any_spec = pl.BlockSpec(memory_space=pl.ANY)
    return pl.pallas_call(
        functools.partial(gather_kernel, z_count, chunks, len(shards)),
        name="gather_weights",
        out_shape=tuple(
            jax.ShapeDtypeStruct((2, z_count, 2, 2) + shard.shape, shard.dtype) for shard in shards
        ),
        in_specs=[any_spec] * len(shards),
        out_specs=[any_spec] * len(shards),
        scratch_shapes=[
            pltpu.SemaphoreType.DMA((pieces,)),
            pltpu.SemaphoreType.DMA((pieces, z_count - 1)),
            pltpu.SemaphoreType.DMA((pieces, z_count - 1)),
            pltpu.SemaphoreType.DMA((pieces, 3)),
            pltpu.SemaphoreType.DMA((pieces, 3)),
        ],
        compiler_params=pltpu.CompilerParams(
            collective_id=0, has_side_effects=True, vmem_limit_bytes=1024 * 1024
        ),
    )(*shards)


def scatter_kernel(z_count, chunks, item_count, *refs):
    grads = refs[:item_count]
    outs = refs[item_count : 2 * item_count]
    scratch = refs[2 * item_count :]
    held = scratch[:item_count]
    from_core = scratch[item_count : 2 * item_count]
    pieces = [piece for chunk in chunks for piece in chunk]
    number = {piece: index for index, piece in enumerate(pieces)}
    total = len(pieces)
    rest = scratch[2 * item_count :]
    from_first = rest[:total]
    from_second = rest[total : 2 * total]
    from_z = rest[2 * total : 3 * total]
    local_sem, z_send, z_recv, hop_send, hop_recv = rest[3 * total :]
    place = Place(z_count)
    x, z, y, c = place.x, place.z, place.y, place.c
    every = slice(None)

    def columns(piece):
        item, lo, hi, unused = piece
        return (every, pl.ds(lo, hi - lo))

    def local_copy(piece):
        item = piece[0]
        return pltpu.make_async_copy(
            grads[item].at[(every, every, every, c) + columns(piece)],
            held[item].at[(every, every, every) + columns(piece)],
            local_sem.at[number[piece]],
        )

    def core_hop(piece):
        item = piece[0]
        return remote(
            grads[item].at[(every, every, every, 1 - c) + columns(piece)],
            from_core[item].at[(every, every, every) + columns(piece)],
            hop_send.at[number[piece], 0],
            hop_recv.at[number[piece], 0],
            place.core_mate(),
        )

    def first_hop(piece):
        item, lo, hi, x_first = piece
        n = number[piece]
        if x_first:
            where, mate = (1 - x, every, every), place.x_mate()
        else:
            where, mate = (every, every, 1 - y), place.y_mate()
        return remote(
            held[item].at[where + columns(piece)],
            from_first[n],
            hop_send.at[n, 1],
            hop_recv.at[n, 1],
            mate,
        )

    def second_hop(piece):
        item, lo, hi, x_first = piece
        n = number[piece]
        if x_first:
            where, mate = (x, every, 1 - y), place.y_mate()
        else:
            where, mate = (1 - x, every, y), place.x_mate()
        return remote(
            held[item].at[where + columns(piece)],
            from_second[n],
            hop_send.at[n, 2],
            hop_recv.at[n, 2],
            mate,
        )

    def z_copy(piece, step):
        n = number[piece]
        return remote(
            held[piece[0]].at[(x, place.z_plus(step), y) + columns(piece)],
            from_z[n].at[step - 1],
            z_send.at[n, step - 1],
            z_recv.at[n, step - 1],
            place.z_mate(step),
        )

    def add_into(ref, where, other):
        dtype = ref.dtype
        value = ref[where].astype(jnp.float32) + other.astype(jnp.float32)
        ref[where] = value.astype(dtype)

    def add_core(piece):
        item = piece[0]

        @pl.loop(0, z_count)
        def _(k):
            for i in range(2):
                for j in range(2):
                    where = (i, k, j) + columns(piece)
                    add_into(held[item], where, from_core[item][where])

    def add_first(piece):
        item, lo, hi, x_first = piece
        n = number[piece]

        @pl.loop(0, z_count)
        def _(k):
            for i in range(2):
                where = ((x, k, i) if x_first else (i, k, y)) + columns(piece)
                add_into(held[item], where, from_first[n][(k, i) if x_first else (i, k)])

    def add_second(piece):
        n = number[piece]

        @pl.loop(0, z_count)
        def _(k):
            where = (x, k, y) + columns(piece)
            add_into(held[piece[0]], where, from_second[n][k])

    def finish(piece):
        item = piece[0]
        n = number[piece]
        value = held[item][(x, z, y) + columns(piece)].astype(jnp.float32)
        for step in range(1, z_count):
            value = value + from_z[n][step - 1].astype(jnp.float32)
        outs[item][columns(piece)] = value

    greet(place)
    count = len(chunks)
    ahead = 2

    def start_core(chunk):
        for piece in chunk:
            local_copy(piece).start()
            core_hop(piece).start()

    for t in range(min(ahead, count)):
        start_core(chunks[t])
    for t in range(count + 3):
        if t + ahead < count:
            start_core(chunks[t + ahead])
        if t < count:
            for piece in chunks[t]:
                local_copy(piece).wait()
                core_hop(piece).wait_recv()
                add_core(piece)
                first_hop(piece).start()
        if 0 <= t - 1 < count:
            for piece in chunks[t - 1]:
                first_hop(piece).wait_recv()
                add_first(piece)
                second_hop(piece).start()
        if 0 <= t - 2 < count:
            for piece in chunks[t - 2]:
                second_hop(piece).wait_recv()
                add_second(piece)
                for step in range(1, z_count):
                    z_copy(piece, step).start()
        if 0 <= t - 3 < count:
            for piece in chunks[t - 3]:
                for step in range(1, z_count):
                    z_copy(piece, step).wait_recv()
                finish(piece)
    for piece in pieces:
        core_hop(piece).wait_send()
        first_hop(piece).wait_send()
        second_hop(piece).wait_send()
        for step in range(1, z_count):
            z_copy(piece, step).wait_send()


def scatter_grads(z_count, grads, chunks):
    pieces = [piece for chunk in chunks for piece in chunk]
    any_spec = pl.BlockSpec(memory_space=pl.ANY)
    tails = [grad.shape[4:] for grad in grads]

    def narrow(piece):
        item, lo, hi, unused = piece
        return (tails[item][0], hi - lo), grads[item].dtype

    scratch = [pltpu.VMEM((2, z_count, 2) + tail, grad.dtype) for grad, tail in zip(grads, tails)]
    scratch += [pltpu.VMEM((2, z_count, 2) + tail, grad.dtype) for grad, tail in zip(grads, tails)]
    for piece in pieces:
        tail, dtype = narrow(piece)
        lead = (z_count, 2) if piece[3] else (2, z_count)
        scratch.append(pltpu.VMEM(lead + tail, dtype))
    for piece in pieces:
        tail, dtype = narrow(piece)
        scratch.append(pltpu.VMEM((z_count,) + tail, dtype))
    for piece in pieces:
        tail, dtype = narrow(piece)
        scratch.append(pltpu.VMEM((z_count - 1,) + tail, dtype))
    count = len(pieces)
    scratch += [
        pltpu.SemaphoreType.DMA((count,)),
        pltpu.SemaphoreType.DMA((count, z_count - 1)),
        pltpu.SemaphoreType.DMA((count, z_count - 1)),
        pltpu.SemaphoreType.DMA((count, 3)),
        pltpu.SemaphoreType.DMA((count, 3)),
    ]
    return pl.pallas_call(
        functools.partial(scatter_kernel, z_count, chunks, len(grads)),
        name="scatter_grads",
        out_shape=tuple(jax.ShapeDtypeStruct(tail, jnp.float32) for tail in tails),
        in_specs=[any_spec] * len(grads),
        out_specs=[pl.BlockSpec(memory_space=pltpu.VMEM)] * len(grads),
        scratch_shapes=scratch,
        compiler_params=pltpu.CompilerParams(
            collective_id=1, has_side_effects=True, vmem_limit_bytes=VMEM_BYTES
        ),
    )(*grads)


def layer_chunks(base, width, ff_width):
    half = (ff_width // 2) // 128 * 128
    cut = (width // 2) // 128 * 128
    return [
        [(base, 0, width, True), (base + 1, 0, width, False)],
        [(base + 2, 0, width, True), (base + 3, 0, width, False)],
        [(base + 4, 0, half, True), (base + 5, 0, half, False)],
        [(base + 4, half, ff_width, True), (base + 5, half, ff_width, False)],
        [(base + 6, 0, cut, True), (base + 6, cut, width, False)],
    ]


def body(
    z_count,
    tokens,
    doc_ids,
    live_mask,
    w_query,
    w_key,
    w_value,
    w_out,
    w_gate,
    w_up,
    w_down,
    gain_attn,
    gain_ffn,
    cotangent,
):
    position, allowed = sequence_layout(doc_ids, live_mask)
    cosine, sine_table = rope_tables(position)
    stacked_weights = (w_query, w_key, w_value, w_out, w_gate, w_up, w_down)
    width, ff_width = w_query.shape[2], w_gate.shape[2]

    gain_rows = gain_attn.shape[1]
    gains = jnp.concatenate([gain_attn, gain_ffn], axis=0).astype(jnp.float32).reshape(-1)
    gain_pad = -gains.shape[0] % 1024
    gain_block = jnp.pad(gains, (0, gain_pad)).reshape(-1, 128)
    shards = [weight[layer] for layer in (0, 1) for weight in stacked_weights] + [gain_block]
    chunks = layer_chunks(0, width, ff_width) + layer_chunks(7, width, ff_width)
    chunks[0] = [(14, 0, 128, True)] + chunks[0]
    gathered = gather_weights(z_count, shards, chunks)
    device_count = z_count * 8
    full_gains = gathered[14].reshape(device_count, -1)[:, : 4 * gain_rows]
    full_gains = full_gains.reshape(device_count, 4, gain_rows).transpose(1, 0, 2).reshape(4, -1)
    full_gains = full_gains.astype(jnp.bfloat16)

    def layer_params(layer):
        matrices = gathered[7 * layer : 7 * layer + 7]
        whole = tuple(matrix.reshape(-1, matrix.shape[-1]) for matrix in matrices)
        return whole + (full_gains[layer], full_gains[2 + layer])

    def reduce_layer(grads):
        low = [grad.astype(jnp.bfloat16) for grad in grads[:7]]
        split = [grad.reshape(2, z_count, 2, 2, -1, grad.shape[-1]) for grad in low]
        gain_grads = jnp.stack(grads[7:9]).reshape(2, device_count, gain_rows)
        gain_grads = gain_grads.transpose(1, 0, 2).reshape(device_count, 2 * gain_rows)
        pad = -2 * gain_rows % 1024
        gain_grads = jnp.pad(gain_grads, ((0, 0), (0, pad)))
        split.append(gain_grads.reshape(2, z_count, 2, 2, -1, 128))
        order = layer_chunks(0, width, ff_width)[::-1]
        order[-1] = order[-1] + [(7, 0, 128, True)]
        sums = scatter_grads(z_count, split, order)
        gain_sums = sums[7].reshape(-1)[: 2 * gain_rows].reshape(2, gain_rows)
        return tuple(sums[:7]) + (gain_sums[0], gain_sums[1])

    params_one = layer_params(0)
    middle_rows, values_first, saved_one = layer_forward(
        tokens.astype(jnp.float32), params_one, None, allowed, cosine, sine_table
    )
    params_two = layer_params(1)
    result, unused_values, saved_two = layer_forward(
        middle_rows, params_two, values_first, allowed, cosine, sine_table
    )
    live_rows = live_mask.astype(jnp.float32)[:, None]
    output = (live_rows * result).astype(jnp.bfloat16)
    grad_result = cotangent.astype(jnp.float32) * live_rows
    grad_middle_rows, grads_two, carried = layer_backward(
        grad_result, params_two, saved_two, None, True, allowed, cosine, sine_table
    )
    shards_two = reduce_layer(grads_two)
    grad_hidden, grads_one, unused_carry = layer_backward(
        grad_middle_rows, params_one, saved_one, carried, False, allowed, cosine, sine_table
    )
    shards_one = reduce_layer(grads_one)
    stacked = tuple(jnp.stack([one, two]) for one, two in zip(shards_one, shards_two))
    return (output, grad_hidden.astype(jnp.bfloat16)) + stacked


def solution(mesh):
    in_specs = (
        P(("dp", "fsdp"), None),
        P(("dp", "fsdp")),
        P(("dp", "fsdp")),
        P(None, ("dp", "fsdp"), None),
        P(None, ("dp", "fsdp"), None),
        P(None, ("dp", "fsdp"), None),
        P(None, ("dp", "fsdp"), None),
        P(None, ("dp", "fsdp"), None),
        P(None, ("dp", "fsdp"), None),
        P(None, ("dp", "fsdp"), None),
        P(None, ("dp", "fsdp")),
        P(None, ("dp", "fsdp")),
        P(("dp", "fsdp"), None),
    )
    out_specs = (
        P(("dp", "fsdp"), None),
        P(("dp", "fsdp"), None),
        P(None, ("dp", "fsdp"), None),
        P(None, ("dp", "fsdp"), None),
        P(None, ("dp", "fsdp"), None),
        P(None, ("dp", "fsdp"), None),
        P(None, ("dp", "fsdp"), None),
        P(None, ("dp", "fsdp"), None),
        P(None, ("dp", "fsdp"), None),
        P(None, ("dp", "fsdp")),
        P(None, ("dp", "fsdp")),
    )
    run = functools.partial(body, mesh.shape["fsdp"] // 4)
    return jax.shard_map(run, mesh=mesh, in_specs=in_specs, out_specs=out_specs, check_vma=False)
```

```python
import functools
import itertools
import math

import jax
import jax.numpy as jnp
from jax import lax
from jax.experimental import pallas as pl
from jax.experimental.pallas import tpu as pltpu
from jax.sharding import PartitionSpec as P

H = 16
HD = 64


EPSILON = 1e-06
ROPE_BASE = 10000.0
MASKED = -1000000000.0


def matmul(left, right):
    return jnp.dot(left, right, preferred_element_type=jnp.float32)


def inner_rows(left, right):
    return lax.dot_general(
        left, right, (((0,), (0,)), ((), ())), preferred_element_type=jnp.float32
    )


def times_transposed(left, right):
    return lax.dot_general(
        left, right, (((1,), (1,)), ((), ())), preferred_element_type=jnp.float32
    )


def sequence_layout(doc_ids, live_mask):
    row_count = doc_ids.shape[0]
    earlier = jnp.sum((doc_ids[None, :] < doc_ids[:, None]).astype(jnp.int32), axis=1)
    row_index = jnp.arange(row_count, dtype=jnp.int32)
    position = row_index - earlier
    allowed = (row_index[None, :] == row_index[:, None]) | (
        row_index[None, :] < row_index[:, None]
    ) & (doc_ids[None, :] == doc_ids[:, None]) & (live_mask[None, :] > 0)
    return (position, allowed)


def rope_tables(position):
    freq_table = ROPE_BASE ** (-jnp.arange(HD // 2, dtype=jnp.float32) * 2.0 / HD)
    angles = position.astype(jnp.float32)[:, None] * freq_table[None, :]
    return (jnp.cos(angles), jnp.sin(angles))


def rotate(matrix, cosine, sine_table, direction):
    row_count = matrix.shape[0]
    heads = matrix.reshape(row_count, H, HD)
    first_half = heads[..., : HD // 2]
    second_half = heads[..., HD // 2 :]
    cos_part = cosine[:, None, :]
    sin_part = direction * sine_table[:, None, :]
    turned = jnp.concatenate(
        [
            first_half * cos_part - second_half * sin_part,
            second_half * cos_part + first_half * sin_part,
        ],
        axis=-1,
    )
    return turned.reshape(row_count, H * HD)


def rms_scale(hidden):
    return lax.rsqrt(jnp.mean(hidden * hidden, axis=1, keepdims=True) + EPSILON)


def norm_backward(grad_normed, unit_rows, inverse_rms, gain_row):
    grad_gain = jnp.sum(grad_normed * unit_rows, axis=0)
    grad_unit = grad_normed * gain_row.astype(jnp.float32)[None, :]
    grad_input = inverse_rms * (
        grad_unit - unit_rows * jnp.mean(grad_unit * unit_rows, axis=1, keepdims=True)
    )
    return (grad_gain, grad_input)


def attention_forward(query_rot, key_rot, mixed_low, allowed):
    row_count = query_rot.shape[0]
    query_heads = query_rot.reshape(row_count, H, HD)
    key_heads = key_rot.reshape(row_count, H, HD)
    value_heads = mixed_low.reshape(row_count, H, HD)
    scores = jnp.einsum(
        "qhd,khd->hqk", query_heads, key_heads, preferred_element_type=jnp.float32
    ) * HD ** (-0.5)
    scores = jnp.where(allowed[None], scores, MASKED)
    row_max = jnp.max(scores, axis=2, keepdims=True)
    weights = jnp.exp(scores - row_max)
    total = jnp.sum(weights, axis=2, keepdims=True)
    prob_low = (weights / total).astype(jnp.bfloat16)
    context = jnp.einsum("hqk,khd->qhd", prob_low, value_heads, preferred_element_type=jnp.float32)
    return (context.reshape(row_count, H * HD), row_max + jnp.log(total))


def attention_backward(query_rot, key_rot, mixed_low, log_norm, allowed, grad_context):
    row_count = query_rot.shape[0]
    query_heads = query_rot.reshape(row_count, H, HD)
    key_heads = key_rot.reshape(row_count, H, HD)
    value_heads = mixed_low.reshape(row_count, H, HD)
    grad_heads = grad_context.reshape(row_count, H, HD)
    scores = jnp.einsum(
        "qhd,khd->hqk", query_heads, key_heads, preferred_element_type=jnp.float32
    ) * HD ** (-0.5)
    attn_prob = jnp.where(allowed[None], jnp.exp(scores - log_norm), 0.0)
    prob_low = attn_prob.astype(jnp.bfloat16)
    grad_mixed = jnp.einsum(
        "hqk,qhd->khd", prob_low, grad_heads, preferred_element_type=jnp.float32
    )
    grad_prob = jnp.einsum(
        "qhd,khd->hqk", grad_heads, value_heads, preferred_element_type=jnp.float32
    )
    row_inner = jnp.sum(attn_prob * grad_prob, axis=2, keepdims=True)
    grad_scores = (attn_prob * (grad_prob - row_inner)).astype(jnp.bfloat16)
    grad_query_rot = jnp.einsum(
        "hqk,khd->qhd", grad_scores, key_heads, preferred_element_type=jnp.float32
    ) * HD ** (-0.5)
    grad_key_rot = jnp.einsum(
        "hqk,qhd->khd", grad_scores, query_heads, preferred_element_type=jnp.float32
    ) * HD ** (-0.5)
    return (
        grad_query_rot.reshape(row_count, H * HD),
        grad_key_rot.reshape(row_count, H * HD),
        grad_mixed.reshape(row_count, H * HD),
    )


def layer_forward(hidden, params, values_first, allowed, cosine, sine_table):
    (
        query_weight,
        key_weight,
        value_weight,
        out_weight,
        gate_weight,
        up_weight,
        down_weight,
        attn_gain,
        ffn_gain,
    ) = params
    inverse_one = rms_scale(hidden)
    unit_one = hidden * inverse_one
    normed_one = (unit_one * attn_gain.astype(jnp.float32)[None, :]).astype(jnp.bfloat16)
    query = matmul(normed_one, query_weight)
    key_rows = matmul(normed_one, key_weight)
    values = matmul(normed_one, value_weight)
    if values_first is None:
        mixed = values
    else:
        mixed = 0.5 * values + 0.5 * values_first
    mixed_low = mixed.astype(jnp.bfloat16)
    query_rot = rotate(query, cosine, sine_table, 1.0).astype(jnp.bfloat16)
    key_rot = rotate(key_rows, cosine, sine_table, 1.0).astype(jnp.bfloat16)
    context, log_norm = attention_forward(query_rot, key_rot, mixed_low, allowed)
    context_low = context.astype(jnp.bfloat16)
    middle = hidden + matmul(context_low, out_weight)
    inverse_two = rms_scale(middle)
    unit_two = middle * inverse_two
    normed_two = (unit_two * ffn_gain.astype(jnp.float32)[None, :]).astype(jnp.bfloat16)
    gate = matmul(normed_two, gate_weight)
    up_part = matmul(normed_two, up_weight)
    hidden_ffn = (jax.nn.silu(gate) * up_part).astype(jnp.bfloat16)
    result = middle + matmul(hidden_ffn, down_weight)
    saved = (
        inverse_one,
        unit_one,
        normed_one,
        mixed_low,
        query_rot,
        key_rot,
        log_norm,
        context_low,
        inverse_two,
        unit_two,
        normed_two,
        gate,
        up_part,
        hidden_ffn,
    )
    return (result, values, saved)


def layer_backward(grad_result, params, saved, carried_in, is_later, allowed, cosine, sine_table):
    (
        query_weight,
        key_weight,
        value_weight,
        out_weight,
        gate_weight,
        up_weight,
        down_weight,
        attn_gain,
        ffn_gain,
    ) = params
    (
        inverse_one,
        unit_one,
        normed_one,
        mixed_low,
        query_rot,
        key_rot,
        log_norm,
        context_low,
        inverse_two,
        unit_two,
        normed_two,
        gate,
        up_part,
        hidden_ffn,
    ) = saved
    grad_down_in = grad_result.astype(jnp.bfloat16)
    grad_w_down = inner_rows(hidden_ffn, grad_down_in)
    grad_ffn_hidden = times_transposed(grad_down_in, down_weight)
    sigma = jax.nn.sigmoid(gate)
    grad_gate = (grad_ffn_hidden * up_part * sigma * (1.0 + gate * (1.0 - sigma))).astype(
        jnp.bfloat16
    )
    grad_up = (grad_ffn_hidden * gate * sigma).astype(jnp.bfloat16)
    grad_w_gate = inner_rows(normed_two, grad_gate)
    grad_w_up = inner_rows(normed_two, grad_up)
    grad_normed_two = times_transposed(grad_gate, gate_weight) + times_transposed(
        grad_up, up_weight
    )
    grad_gain_ffn, grad_from_norm = norm_backward(grad_normed_two, unit_two, inverse_two, ffn_gain)
    grad_middle = grad_result + grad_from_norm
    grad_branch = grad_middle.astype(jnp.bfloat16)
    grad_w_out = inner_rows(context_low, grad_branch)
    grad_context = times_transposed(grad_branch, out_weight).astype(jnp.bfloat16)
    grad_query_rot, grad_key_rot, grad_mixed = attention_backward(
        query_rot, key_rot, mixed_low, log_norm, allowed, grad_context
    )
    grad_query = rotate(grad_query_rot, cosine, sine_table, -1.0).astype(jnp.bfloat16)
    grad_key = rotate(grad_key_rot, cosine, sine_table, -1.0).astype(jnp.bfloat16)
    if is_later:
        grad_values = (0.5 * grad_mixed).astype(jnp.bfloat16)
        carried = 0.5 * grad_mixed
    else:
        grad_values = (grad_mixed + carried_in).astype(jnp.bfloat16)
        carried = None
    grad_w_query = inner_rows(normed_one, grad_query)
    grad_w_key = inner_rows(normed_one, grad_key)
    grad_w_value = inner_rows(normed_one, grad_values)
    grad_normed_one = (
        times_transposed(grad_query, query_weight)
        + times_transposed(grad_key, key_weight)
        + times_transposed(grad_values, value_weight)
    )
    grad_gain_attn, grad_from_first = norm_backward(
        grad_normed_one, unit_one, inverse_one, attn_gain
    )
    grad_hidden = grad_middle + grad_from_first
    grads = (
        grad_w_query,
        grad_w_key,
        grad_w_value,
        grad_w_out,
        grad_w_gate,
        grad_w_up,
        grad_w_down,
        grad_gain_attn,
        grad_gain_ffn,
    )
    return (grad_hidden, grads, carried)


MESH_ID = pl.DeviceIdType.MESH
VMEM_BYTES = 127 * 512 * 1024


class Place:
    def __init__(self, z_count):
        self.z_count = z_count
        self.x = lax.axis_index("dp")
        f = lax.axis_index("fsdp")
        self.z = f // 4
        self.y = lax.rem(f, 4) // 2
        self.c = lax.rem(f, 2)

    def device(self, x, z, y, c):
        return (x, z * 4 + y * 2 + c)

    def x_mate(self):
        return self.device(1 - self.x, self.z, self.y, self.c)

    def y_mate(self):
        return self.device(self.x, self.z, 1 - self.y, self.c)

    def core_mate(self):
        return self.device(self.x, self.z, self.y, 1 - self.c)

    def z_plus(self, step):
        return lax.rem(self.z + step, self.z_count)

    def z_minus(self, step):
        return lax.rem(self.z + self.z_count - step, self.z_count)

    @property
    def relays(self):
        return self.z_count == 4

    def is_middle(self):
        return (self.z == 1) | (self.z == 2)

    def z_targets(self):
        if not self.relays:
            return [self.z_plus(step) for step in range(1, self.z_count)]
        z = self.z
        return [lax.rem(z + 3, 4) - 2 * ((3 - z) // 3), 2 + z // 2 * (5 - 2 * z)]

    def z_mate(self, step):
        return self.device(self.x, self.z_plus(step), self.y, self.c)


def greet(place):
    barrier = pltpu.get_barrier_semaphore()
    mates = [place.x_mate(), place.y_mate(), place.core_mate()]
    mates += [place.z_mate(k) for k in range(1, place.z_count)]
    for mate in mates:
        pl.semaphore_signal(barrier, inc=1, device_id=mate, device_id_type=MESH_ID)
    pl.semaphore_wait(barrier, len(mates))


def remote(src, dst, send_sem, recv_sem, device):
    return pltpu.make_async_remote_copy(
        src_ref=src,
        dst_ref=dst,
        send_sem=send_sem,
        recv_sem=recv_sem,
        device_id=device,
        device_id_type=MESH_ID,
    )


class Gather:
    STEPS = 6

    def __init__(self, z_count, chunks, shards, outs, semaphores):
        self.place = Place(z_count)
        self.shards, self.outs = shards, outs
        self.pieces = [piece for chunk in chunks for piece in chunk]
        self.number = {piece: index for index, piece in enumerate(self.pieces)}
        (
            self.local_sem,
            self.z_send,
            self.z_recv,
            self.relay_send,
            self.relay_recv,
            self.hop_send,
            self.hop_recv,
        ) = semaphores

    def window(self, piece, where):
        item, lo, hi, unused = piece
        return self.outs[item].at[tuple(where) + (slice(None), pl.ds(lo, hi - lo))]

    def own(self, piece):
        item, lo, hi, unused = piece
        return self.shards[item].at[:, pl.ds(lo, hi - lo)]

    def region(self, piece, axis, value):
        place = self.place
        done = piece[3][: piece[3].index(axis)] if axis != "c" else "xyz"
        where = {"x": place.x, "z": place.z, "y": place.y, "c": place.c}
        for name in done:
            where[name] = slice(None)
        where[axis] = value
        return self.window(piece, (where["x"], where["z"], where["y"], where["c"]))

    def local_copy(self, piece):
        place = self.place
        target = self.window(piece, (place.x, place.z, place.y, place.c))
        return pltpu.make_async_copy(
            self.own(piece), target, self.local_sem.at[self.number[piece]]
        )

    def source(self, piece, axis, value):
        return self.own(piece) if piece[3][0] == axis else self.region(piece, axis, value)

    def z_copies(self, piece):
        place, n = self.place, self.number[piece]
        return [
            remote(
                self.source(piece, "z", place.z),
                self.region(piece, "z", place.z),
                self.z_send.at[n, index],
                self.z_recv.at[n, place.z],
                place.device(place.x, target, place.y, place.c),
            )
            for index, target in enumerate(place.z_targets())
        ]

    def z_arrival(self, piece, source_z):
        place, n = self.place, self.number[piece]
        ref = self.region(piece, "z", source_z)
        return remote(
            ref,
            ref,
            self.z_send.at[n, 0],
            self.z_recv.at[n, source_z],
            place.device(place.x, source_z, place.y, place.c),
        )

    def relay(self, piece, arriving):
        place, n = self.place, self.number[piece]
        if arriving:
            first, target = 2 - 2 * (place.z // 3), 1 + place.z // 3
        else:
            first, target = 2 * (2 - place.z), 3 * (place.z - 1)
        ref = self.region(piece, "z", pl.ds(first, 2))
        return remote(
            ref,
            ref,
            self.relay_send.at[n],
            self.relay_recv.at[n],
            place.device(place.x, target, place.y, place.c),
        )

    def hop(self, piece, axis, arriving):
        place = self.place
        own = {"x": place.x, "y": place.y, "c": place.c}[axis]
        mate = {"x": place.x_mate, "y": place.y_mate, "c": place.core_mate}[axis]()
        n, index = self.number[piece], "xyc".index(axis)
        target = self.region(piece, axis, 1 - own if arriving else own)
        source = target if arriving else self.source(piece, axis, own)
        return remote(
            source, target, self.hop_send.at[n, index], self.hop_recv.at[n, index], mate
        )

    def begin(self, piece, axis):
        if axis == "z":
            for copy in self.z_copies(piece):
                copy.start()
        else:
            self.hop(piece, axis, False).start()

    def pass_on(self, piece):
        place = self.place
        if not place.relays:
            return

        @pl.when(place.is_middle())
        def _():
            for step in range(1, place.z_count):
                self.z_arrival(piece, place.z_plus(step)).wait_recv()
            self.relay(piece, False).start()

    def end(self, piece, axis):
        place = self.place
        if axis != "z":
            self.hop(piece, axis, True).wait_recv()
        elif place.relays:

            @pl.when(jnp.logical_not(place.is_middle()))
            def _():
                self.z_arrival(piece, 1 + place.z // 3).wait_recv()
                self.relay(piece, True).wait_recv()

        else:
            for step in range(1, place.z_count):
                self.z_arrival(piece, place.z_plus(step)).wait_recv()

    def step(self, chunk, index):
        for piece in chunk:
            order = piece[3]
            actions = []
            for axis in order + "c":
                actions.append(("begin", axis))
                if axis == "z":
                    actions.append(("relay", axis))
            kind, axis = actions[index] if index < len(actions) else ("done", "c")
            if index == 0:
                self.local_copy(piece).start()
                self.begin(piece, axis)
                continue
            last_kind, last_axis = actions[index - 1]
            if kind == "relay":
                self.pass_on(piece)
                continue
            self.end(piece, last_axis)
            if order[0] == last_axis:
                self.local_copy(piece).wait()
            if kind == "begin":
                self.begin(piece, axis)

    def close(self):
        place = self.place
        for piece in self.pieces:
            for copy in self.z_copies(piece):
                copy.wait_send()
            for axis in "xyc":
                self.hop(piece, axis, False).wait_send()
            if place.relays:

                @pl.when(place.is_middle())
                def _(piece=piece):
                    self.relay(piece, False).wait_send()


def gather_semaphores(pieces, z_count):
    return [
        pltpu.SemaphoreType.DMA((pieces,)),
        pltpu.SemaphoreType.DMA((pieces, z_count - 1)),
        pltpu.SemaphoreType.DMA((pieces, z_count)),
        pltpu.SemaphoreType.DMA((pieces,)),
        pltpu.SemaphoreType.DMA((pieces,)),
        pltpu.SemaphoreType.DMA((pieces, 3)),
        pltpu.SemaphoreType.DMA((pieces, 3)),
    ]


def gather_kernel(z_count, chunks, item_count, *refs):
    gather = Gather(
        z_count, chunks, refs[:item_count], refs[item_count : 2 * item_count], refs[2 * item_count :]
    )
    greet(gather.place)
    for tick in range(len(chunks) + AHEAD_LAGS[-1]):
        for step in range(Gather.STEPS - 1, -1, -1):
            index = tick - AHEAD_LAGS[step]
            if 0 <= index < len(chunks):
                gather.step(chunks[index], step)
    gather.close()


def gather_weights(z_count, shards, chunks):
    pieces = sum(len(chunk) for chunk in chunks)
    any_spec = pl.BlockSpec(memory_space=pl.ANY)
    return pl.pallas_call(
        functools.partial(gather_kernel, z_count, chunks, len(shards)),
        name="gather_weights",
        out_shape=tuple(
            jax.ShapeDtypeStruct((2, z_count, 2, 2) + shard.shape, shard.dtype) for shard in shards
        ),
        in_specs=[any_spec] * len(shards),
        out_specs=[any_spec] * len(shards),
        scratch_shapes=gather_semaphores(pieces, z_count),
        compiler_params=pltpu.CompilerParams(
            collective_id=0, has_side_effects=True, vmem_limit_bytes=1024 * 1024
        ),
    )(*shards)


def scatter_kernel(z_count, chunks, item_count, *refs):
    grads = refs[:item_count]
    outs = refs[item_count : 2 * item_count]
    scratch = refs[2 * item_count :]
    held = scratch[:item_count]
    from_core = scratch[item_count : 2 * item_count]
    pieces = [piece for chunk in chunks for piece in chunk]
    number = {piece: index for index, piece in enumerate(pieces)}
    total = len(pieces)
    rest = scratch[2 * item_count :]
    from_first = rest[:total]
    from_second = rest[total : 2 * total]
    from_z = rest[2 * total : 3 * total]
    local_sem, z_send, z_recv, hop_send, hop_recv = rest[3 * total :]
    place = Place(z_count)
    x, z, y, c = place.x, place.z, place.y, place.c
    every = slice(None)

    def columns(piece):
        item, lo, hi, unused = piece
        return (every, pl.ds(lo, hi - lo))

    def local_copy(piece):
        item = piece[0]
        return pltpu.make_async_copy(
            grads[item].at[(every, every, every, c) + columns(piece)],
            held[item].at[(every, every, every) + columns(piece)],
            local_sem.at[number[piece]],
        )

    def core_hop(piece):
        item = piece[0]
        return remote(
            grads[item].at[(every, every, every, 1 - c) + columns(piece)],
            from_core[item].at[(every, every, every) + columns(piece)],
            hop_send.at[number[piece], 0],
            hop_recv.at[number[piece], 0],
            place.core_mate(),
        )

    def first_hop(piece):
        item, lo, hi, x_first = piece
        n = number[piece]
        if x_first:
            where, mate = (1 - x, every, every), place.x_mate()
        else:
            where, mate = (every, every, 1 - y), place.y_mate()
        return remote(
            held[item].at[where + columns(piece)],
            from_first[n],
            hop_send.at[n, 1],
            hop_recv.at[n, 1],
            mate,
        )

    def second_hop(piece):
        item, lo, hi, x_first = piece
        n = number[piece]
        if x_first:
            where, mate = (x, every, 1 - y), place.y_mate()
        else:
            where, mate = (1 - x, every, y), place.x_mate()
        return remote(
            held[item].at[where + columns(piece)],
            from_second[n],
            hop_send.at[n, 2],
            hop_recv.at[n, 2],
            mate,
        )

    def z_copy(piece, step):
        n = number[piece]
        return remote(
            held[piece[0]].at[(x, place.z_plus(step), y) + columns(piece)],
            from_z[n].at[step - 1],
            z_send.at[n, step - 1],
            z_recv.at[n, step - 1],
            place.z_mate(step),
        )

    def add_into(ref, where, other):
        dtype = ref.dtype
        value = ref[where].astype(jnp.float32) + other.astype(jnp.float32)
        ref[where] = value.astype(dtype)

    def add_core(piece):
        item = piece[0]

        @pl.loop(0, z_count)
        def _(k):
            for i in range(2):
                for j in range(2):
                    where = (i, k, j) + columns(piece)
                    add_into(held[item], where, from_core[item][where])

    def add_first(piece):
        item, lo, hi, x_first = piece
        n = number[piece]

        @pl.loop(0, z_count)
        def _(k):
            for i in range(2):
                where = ((x, k, i) if x_first else (i, k, y)) + columns(piece)
                add_into(held[item], where, from_first[n][(k, i) if x_first else (i, k)])

    def add_second(piece):
        n = number[piece]

        @pl.loop(0, z_count)
        def _(k):
            where = (x, k, y) + columns(piece)
            add_into(held[piece[0]], where, from_second[n][k])

    def finish(piece):
        item = piece[0]
        n = number[piece]
        value = held[item][(x, z, y) + columns(piece)].astype(jnp.float32)
        for step in range(1, z_count):
            value = value + from_z[n][step - 1].astype(jnp.float32)
        outs[item][columns(piece)] = value

    greet(place)
    count = len(chunks)
    ahead = 2

    def start_core(chunk):
        for piece in chunk:
            local_copy(piece).start()
            core_hop(piece).start()

    for t in range(min(ahead, count)):
        start_core(chunks[t])
    for t in range(count + 3):
        if t + ahead < count:
            start_core(chunks[t + ahead])
        if t < count:
            for piece in chunks[t]:
                local_copy(piece).wait()
                core_hop(piece).wait_recv()
                add_core(piece)
                first_hop(piece).start()
        if 0 <= t - 1 < count:
            for piece in chunks[t - 1]:
                first_hop(piece).wait_recv()
                add_first(piece)
                second_hop(piece).start()
        if 0 <= t - 2 < count:
            for piece in chunks[t - 2]:
                second_hop(piece).wait_recv()
                add_second(piece)
                for step in range(1, z_count):
                    z_copy(piece, step).start()
        if 0 <= t - 3 < count:
            for piece in chunks[t - 3]:
                for step in range(1, z_count):
                    z_copy(piece, step).wait_recv()
                finish(piece)
    for piece in pieces:
        core_hop(piece).wait_send()
        first_hop(piece).wait_send()
        second_hop(piece).wait_send()
        for step in range(1, z_count):
            z_copy(piece, step).wait_send()


def scatter_grads(z_count, grads, chunks):
    pieces = [piece for chunk in chunks for piece in chunk]
    any_spec = pl.BlockSpec(memory_space=pl.ANY)
    tails = [grad.shape[4:] for grad in grads]

    def narrow(piece):
        item, lo, hi, unused = piece
        return (tails[item][0], hi - lo), grads[item].dtype

    scratch = [pltpu.VMEM((2, z_count, 2) + tail, grad.dtype) for grad, tail in zip(grads, tails)]
    scratch += [pltpu.VMEM((2, z_count, 2) + tail, grad.dtype) for grad, tail in zip(grads, tails)]
    for piece in pieces:
        tail, dtype = narrow(piece)
        lead = (z_count, 2) if piece[3] else (2, z_count)
        scratch.append(pltpu.VMEM(lead + tail, dtype))
    for piece in pieces:
        tail, dtype = narrow(piece)
        scratch.append(pltpu.VMEM((z_count,) + tail, dtype))
    for piece in pieces:
        tail, dtype = narrow(piece)
        scratch.append(pltpu.VMEM((z_count - 1,) + tail, dtype))
    count = len(pieces)
    scratch += [
        pltpu.SemaphoreType.DMA((count,)),
        pltpu.SemaphoreType.DMA((count, z_count - 1)),
        pltpu.SemaphoreType.DMA((count, z_count - 1)),
        pltpu.SemaphoreType.DMA((count, 3)),
        pltpu.SemaphoreType.DMA((count, 3)),
    ]
    return pl.pallas_call(
        functools.partial(scatter_kernel, z_count, chunks, len(grads)),
        name="scatter_grads",
        out_shape=tuple(jax.ShapeDtypeStruct(tail, jnp.float32) for tail in tails),
        in_specs=[any_spec] * len(grads),
        out_specs=[pl.BlockSpec(memory_space=pltpu.VMEM)] * len(grads),
        scratch_shapes=scratch,
        compiler_params=pltpu.CompilerParams(
            collective_id=1, has_side_effects=True, vmem_limit_bytes=VMEM_BYTES
        ),
    )(*grads)

def rms_rows(source, gain_row, target):
    @pl.loop(0, source.shape[0] // 64)
    def _(step):
        rows = pl.ds(pl.multiple_of(step * 64, 64), 64)
        value = source[rows, :]
        inverse = lax.rsqrt(jnp.mean(value * value, axis=1, keepdims=True) + EPSILON)
        target[rows, :] = (value * inverse * gain_row).astype(target.dtype)


def transpose_into(source, target):
    @tiles(0, source.shape[1], 256)
    def _(columns):
        target[columns, :] = source[:, columns].T


def swap_halves(block):
    lane = lax.broadcasted_iota(jnp.int32, block.shape, 1)
    ahead = pltpu.roll(block, 96, axis=1)
    behind = pltpu.roll(block, 32, axis=1)
    return jnp.where(lane % 64 < 32, ahead, behind)


def turn(block, cosine, sine):
    return block * cosine + swap_halves(block) * sine


def tiles(start, stop, width):
    def wrap(fn):
        @pl.loop(start // width, stop // width)
        def _(step):
            fn(pl.ds(pl.multiple_of(step * width, width), width))

    return wrap


def attend_pairs(start, stop, query, key, value, mask, context, norms):
    rows = query.shape[0]
    block = rows // 2

    @pl.loop(start, stop)
    def _(pair):
        lanes = pl.ds(pl.multiple_of(pair * 128, 128), 128)
        for q_index in range(2):
            q_rows = pl.ds(q_index * block, block)
            keys = (q_index + 1) * block
            q_block = query[q_rows, lanes]
            k_block = key[0:keys, lanes]
            v_block = value[0:keys, lanes]
            low_half = lax.broadcasted_iota(jnp.int32, (block, 128), 1) < 64
            allowed = mask[q_rows, 0:keys].astype(jnp.float32) > 0
            outs = []
            for head in range(2):
                own = low_half if head == 0 else jnp.logical_not(low_half)
                q_own = jnp.where(own, q_block, jnp.zeros_like(q_block))
                scores = times_transposed(q_own, k_block)
                scores = jnp.where(allowed, scores, MASKED)
                top = jnp.max(scores, axis=1, keepdims=True)
                weights = jnp.exp(scores - top)
                total = jnp.sum(weights, axis=1, keepdims=True)
                prob = (weights * (1.0 / total)).astype(jnp.bfloat16)
                outs.append(matmul(prob, v_block))
                norm = top + jnp.log(total)
                lane = lax.broadcasted_iota(jnp.int32, (block, 128), 1)
                norms[q_rows, :] = jnp.where(lane == 2 * pair + head, norm, norms[q_rows, :])
            context[q_rows, lanes] = jnp.where(low_half, outs[0], outs[1]).astype(context.dtype)


KEPT = ("hid", "n1t", "q", "k", "v", "ctxt", "lse", "mid", "n2t", "g", "u", "ht")
TABLES = ("gains", "mask", "cosine", "sine", "live")
PARTS = 6
AHEAD_LAGS = (0, 2, 4, 6, 8, 10)


def fill_tables(doc_ids, live_mask, mask, cosine, sine, live):
    rows = doc_ids.shape[1]
    doc_row = doc_ids[...].astype(jnp.float32)
    live_row = live_mask[...].astype(jnp.float32)
    doc_wide = jnp.broadcast_to(doc_row, (128, rows)).T
    live[...] = jnp.broadcast_to(live_row, (128, rows)).T
    for first in range(0, rows, 128):
        doc_column = doc_wide[first : first + 128, 0:1]
        earlier = jnp.sum(
            jnp.where(doc_row < doc_column, 1.0, 0.0), axis=1, keepdims=True
        )
        row = lax.broadcasted_iota(jnp.int32, (128, rows), 0) + first
        column = lax.broadcasted_iota(jnp.int32, (128, rows), 1)
        seen = (column < row) & (doc_row == doc_column) & (live_row > 0)
        mask[first : first + 128, :] = jnp.where(seen | (column == row), 1.0, 0.0).astype(mask.dtype)
        lane = lax.broadcasted_iota(jnp.int32, (128, 128), 1)
        slot = lax.broadcasted_iota(jnp.int32, (128, 128), 0) + first
        exponent = (lane % 32).astype(jnp.float32) * (-2.0 / HD)
        angle = (slot.astype(jnp.float32) - earlier) * jnp.exp(exponent * math.log(ROPE_BASE))
        cosine[first : first + 128, :] = jnp.cos(angle)
        sine[first : first + 128, :] = jnp.where(lane % 64 < 32, -1.0, 1.0) * jnp.sin(angle)


def place_gains(blocks, gain_rows, target):
    row_count, width = blocks.shape[0], target.shape[1]
    row = lax.broadcasted_iota(jnp.int32, (row_count, width), 0)
    column = lax.broadcasted_iota(jnp.int32, (row_count, width), 1)
    source = lax.broadcasted_iota(jnp.int32, (128, width), 0)
    lane = lax.broadcasted_iota(jnp.int32, (128, width), 1)
    pick = (source == lane % gain_rows).astype(jnp.bfloat16)
    spread = matmul(blocks[...].astype(jnp.bfloat16), pick)
    for index in range(4):
        own = row == (column // gain_rows) * 8 + index
        target[index : index + 1, :] = jnp.sum(
            jnp.where(own, spread, 0.0), axis=0, keepdims=True
        )


def forward_kernel(z_count, chunks, split, *refs):
    refs = list(refs)

    def take(count):
        taken = refs[:count]
        del refs[:count]
        return taken

    stacked = take(7)
    tokens, doc_ids, live_mask, gain_attn, gain_ffn = take(5)
    outs = take(15)
    saved = [take(len(KEPT)) for unused in (0, 1)]
    table_outs = take(len(TABLES))
    (output,) = take(1)
    buffers = dict(zip((name for name in KEPT if name != "mid"), take(len(KEPT) - 1)))
    buffers["mid"] = mid = buffers["hid"]
    tables = take(len(TABLES))
    gains, mask, cosine, sine, live = tables
    ctx, h, n1, values_first = take(4)
    n2 = n1
    weights = take(9)
    own_gains, gain_block = take(2)
    load_sem, save_sem, table_sem = take(3)
    shards = [stacked[k].at[layer] for layer in (0, 1) for k in range(7)] + [own_gains]
    gather = Gather(z_count, chunks, shards, outs, refs)
    hid, n1t, query, key, value = (buffers[name] for name in ("hid", "n1t", "q", "k", "v"))
    ctxt, lse, n2t, g, u, ht = (buffers[name] for name in ("ctxt", "lse", "n2t", "g", "u", "ht"))
    gain_rows = gain_attn.shape[1]
    ff_width = g.shape[1]
    width = hid.shape[1]

    def save_copy(layer, name):
        index = KEPT.index(name)
        return pltpu.make_async_copy(
            buffers[name], saved[layer][index], save_sem.at[layer, index]
        )

    def save(layer, *names):
        for name in names:
            save_copy(layer, name).start()

    def saved_before(layer, *names):
        for name in names:
            if layer >= 0:
                save_copy(layer, name).wait()

    def table_copies():
        return [
            pltpu.make_async_copy(source, target, table_sem.at[index])
            for index, (source, target) in enumerate(zip(tables, table_outs))
        ]

    def flat(item):
        ref = outs[item]
        return ref.reshape(z_count * 8 * ref.shape[4], ref.shape[5])

    def down_rows(item, columns, target):
        ref = outs[item]
        step = ref.shape[4]
        places = itertools.product(range(2), range(z_count), range(2), range(2))
        return [
            (
                ref.at[where + (slice(None), columns)],
                target.at[pl.ds(index * step, step), columns],
            )
            for index, where in enumerate(places)
        ]

    def loads(layer, part):
        base = 7 * layer
        wq, wk, wv, wo, wg_lo, wu_lo, wg_hi, wu_hi, wd = weights
        every = slice(None)
        if part < 4:
            low, high = pl.ds(0, split), pl.ds(split, ff_width - split)
            pairs = [
                [(flat(base), wq), (flat(base + 1), wk)],
                [(flat(base + 2), wv), (flat(base + 3), wo)],
                [(flat(base + 4).at[every, low], wg_lo), (flat(base + 5).at[every, low], wu_lo)],
                [(flat(base + 4).at[every, high], wg_hi), (flat(base + 5).at[every, high], wu_hi)],
            ][part]
        else:
            half = pl.ds((part - 4) * (width // 2), width // 2)
            pairs = down_rows(base + 6, half, wd)
        copies = [
            pltpu.make_async_copy(source, target, load_sem.at[part, index])
            for index, (source, target) in enumerate(pairs)
        ]
        if part == 0 and layer == 0:
            copies.append(
                pltpu.make_async_copy(
                    outs[14].reshape(gain_block.shape[0], 128), gain_block, load_sem.at[0, 2]
                )
            )
        return copies

    def compute(layer, part):
        wq, wk, wv, wo, wg_lo, wu_lo, wg_hi, wu_hi, wd = weights
        for copy in loads(layer, part):
            copy.wait()
        before = layer - 1
        if part == 0:
            if layer == 0:
                place_gains(gain_block, gain_rows, gains)
                for copy in table_copies():
                    copy.start()
            saved_before(before, "n1t", "q", "k")
            rms_rows(hid, gains[layer : layer + 1, :], n1)
            transpose_into(n1, n1t)
            save(layer, "hid", "n1t")
            yield

            def turned(columns, weight):
                block = matmul(n1[...], weight[:, columns])
                halves = [turn(block[:, s : s + 128], cosine[...], sine[...]) for s in (0, 128)]
                return jnp.concatenate(halves, axis=1).astype(jnp.bfloat16)

            @tiles(0, width, 256)
            def _(columns):
                query[:, columns] = turned(columns, wq) * jnp.asarray(HD ** (-0.5), jnp.bfloat16)

            yield

            @tiles(0, width, 256)
            def _(columns):
                key[:, columns] = turned(columns, wk)

            save(layer, "q", "k")
            yield
        if part == 1:
            saved_before(before, "v", "ctxt", "lse", "n2t")

            @tiles(0, width, 256)
            def _(columns):
                block = matmul(n1[...], wv[:, columns])
                if layer == 0:
                    values_first[:, columns] = block
                    value[:, columns] = block.astype(jnp.bfloat16)
                else:
                    mixed = 0.5 * block + 0.5 * values_first[:, columns]
                    value[:, columns] = mixed.astype(jnp.bfloat16)

            lse[...] = jnp.zeros_like(lse)
            save(layer, "v")
            yield
            for start in range(0, H // 2, 2):
                attend_pairs(start, start + 2, query, key, value, mask, ctx, lse)
                yield
            transpose_into(ctx, ctxt)
            save(layer, "ctxt", "lse")
            saved_before(layer, "hid")

            @tiles(0, width, 256)
            def _(columns):
                mid[:, columns] = hid[:, columns] + matmul(ctx[...], wo[:, columns])

            yield
            rms_rows(mid, gains[layer + 2 : layer + 3, :], n2)
            transpose_into(n2, n2t)
            save(layer, "mid", "n2t")
            yield
        if part in (2, 3):
            if part == 2:
                saved_before(before, "g", "u", "ht")
            start, stop = (0, split) if part == 2 else (split, ff_width)
            w_gate, w_up = (wg_lo, wu_lo) if part == 2 else (wg_hi, wu_hi)
            middle = start + (stop - start) // 512 * 256
            for lo, hi in ((start, middle), (middle, stop)):

                @tiles(lo, hi, 256)
                def _(columns):
                    inner = pl.ds(pl.multiple_of(columns.start - start, 256), 256)
                    gate = matmul(n2[...], w_gate[:, inner])
                    up = matmul(n2[...], w_up[:, inner])
                    g[:, columns] = gate.astype(jnp.bfloat16)
                    u[:, columns] = up.astype(jnp.bfloat16)
                    hidden = (gate * jax.nn.sigmoid(gate) * up).astype(jnp.bfloat16)
                    h[:, columns] = hidden
                    ht[columns, :] = hidden.T

                yield
            if part == 3:
                save(layer, "g", "u", "ht")
        if part >= 4:
            if part == 4:
                saved_before(layer, "mid")
            first = (part - 4) * (width // 2)

            @tiles(first, first + width // 2, 256)
            def _(columns):
                result = mid[:, columns] + matmul(h[...], wd[:, columns])
                if layer == 0:
                    hid[:, columns] = result
                else:
                    output[:, columns] = (result * live[:, 0:1]).astype(jnp.bfloat16)

            yield

    own_gains[...] = jnp.zeros_like(own_gains)
    own_gains[0:2, 0:gain_rows] = gain_attn[...].astype(jnp.float32)
    own_gains[2:4, 0:gain_rows] = gain_ffn[...].astype(jnp.float32)
    greet(gather.place)
    per_layer = len(chunks) // 2
    ready = [layer * per_layer + last for layer in (0, 1) for last in (1, 3, 5, 7, 8, 9)]
    steps_of = (3, 7, 2, 2, 1, 1)
    due = {}
    for index, chunk in enumerate(ready[:-1]):
        slots = [
            (tick, slot)
            for tick in range(chunk + AHEAD_LAGS[-1] + 1, ready[index + 1] + AHEAD_LAGS[-1] + 1)
            for slot in range(6)
        ]
        count = steps_of[index % PARTS]
        for number in range(count):
            slot = slots[number * len(slots) // count]
            due[slot] = due.get(slot, 0) + 1

    def all_steps():
        for index in range(len(ready)):
            yield from compute(index // PARTS, index % PARTS)

    work = all_steps()
    for tick in range(len(chunks) + AHEAD_LAGS[-1]):
        for step in range(Gather.STEPS - 1, -1, -1):
            index = tick - AHEAD_LAGS[step]
            if 0 <= index < len(chunks):
                gather.step(chunks[index], step)
            for unused in range(due.get((tick, 5 - step), 0)):
                next(work, None)
        if tick == 0:
            fill_tables(doc_ids, live_mask, mask, cosine, sine, live)

            @pl.loop(0, hid.shape[0] // 64)
            def _(step):
                rows = pl.ds(pl.multiple_of(step * 64, 64), 64)
                hid[rows, :] = tokens[rows, :].astype(jnp.float32)

        done = tick - AHEAD_LAGS[-1]
        if done in ready:
            part = ready.index(done)
            for copy in loads(part // PARTS, part % PARTS):
                copy.start()
    for unused in work:
        pass
    for copy in table_copies():
        copy.wait()
    for name in KEPT:
        if name not in ("hid", "mid"):
            saved_before(1, name)
    gather.close()


def forward(z_count, stacked, chunks, split, tokens, doc_ids, live_mask, gain_attn, gain_ffn):
    pieces = sum(len(chunk) for chunk in chunks)
    rows, width = tokens.shape
    ff_width = stacked[4].shape[2]
    any_spec = pl.BlockSpec(memory_space=pl.ANY)
    vmem_spec = pl.BlockSpec(memory_space=pltpu.VMEM)
    low, wide = jnp.bfloat16, jnp.float32
    shapes = {name: ((rows, width), low) for name in KEPT}
    shapes["hid"] = shapes["mid"] = ((rows, width), wide)
    shapes["lse"] = ((rows, 128), wide)
    shapes["g"] = shapes["u"] = ((rows, ff_width), low)
    shapes["n1t"] = shapes["n2t"] = shapes["ctxt"] = ((width, rows), low)
    shapes["ht"] = ((ff_width, rows), low)
    tables = {name: ((rows, 128), wide) for name in TABLES}
    tables["gains"] = ((8, width), wide)
    tables["mask"] = ((rows, rows), low)
    depth = z_count * 8 * stacked[0].shape[1]
    shards = [w.shape[1:] for w in stacked] * 2
    gathered = [jax.ShapeDtypeStruct((2, z_count, 2, 2) + shape, low) for shape in shards]
    gathered.append(jax.ShapeDtypeStruct((2, z_count, 2, 2, 8, 128), wide))
    kept = [jax.ShapeDtypeStruct(*shapes[name]) for name in KEPT] * 2
    table_outs = [jax.ShapeDtypeStruct(*tables[name]) for name in TABLES]
    results = pl.pallas_call(
        functools.partial(forward_kernel, z_count, chunks, split),
        name="forward_gather",
        out_shape=tuple(gathered + kept + table_outs) + (jax.ShapeDtypeStruct((rows, width), low),),
        in_specs=[any_spec] * 7 + [vmem_spec] * 5,
        out_specs=[any_spec] * (len(gathered) + len(kept) + len(table_outs)) + [vmem_spec],
        scratch_shapes=[pltpu.VMEM(*shapes[name]) for name in KEPT if name != "mid"]
        + [pltpu.VMEM(*tables[name]) for name in TABLES]
        + [pltpu.VMEM((rows, width), low), pltpu.VMEM((rows, ff_width), low)]
        + [pltpu.VMEM((rows, width), low), pltpu.VMEM((rows, width), wide)]
        + [pltpu.VMEM((depth, width), low)] * 4
        + [pltpu.VMEM((depth, split), low)] * 2
        + [pltpu.VMEM((depth, ff_width - split), low)] * 2
        + [pltpu.VMEM((ff_width, width), low)]
        + [pltpu.VMEM((8, 128), wide), pltpu.VMEM((z_count * 64, 128), wide)]
        + [
            pltpu.SemaphoreType.DMA((PARTS, z_count * 8)),
            pltpu.SemaphoreType.DMA((2, len(KEPT))),
            pltpu.SemaphoreType.DMA((len(TABLES),)),
        ]
        + gather_semaphores(pieces, z_count),
        compiler_params=pltpu.CompilerParams(
            collective_id=2, has_side_effects=True, vmem_limit_bytes=VMEM_BYTES
        ),
    )(*stacked, tokens, doc_ids, live_mask, gain_attn, gain_ffn)
    names = [dict(zip(KEPT, results[15 + len(KEPT) * k :])) for k in (0, 1)]
    at = 15 + 2 * len(KEPT)
    return results[:15], names, results[at : at + len(TABLES)], results[-1]


class Piece:
    def __init__(self, kind, layer, item, lo, hi, x_first, late):
        self.kind, self.layer, self.item = kind, layer, item
        self.lo, self.hi, self.x_first, self.late = lo, hi, x_first, late
        self.index = self.order = self.done = self.moved = 0
        self.slots = {}

    @property
    def width(self):
        return self.hi - self.lo

    @property
    def ops(self):
        return LATE_OPS if self.late else EARLY_OPS


DOWN_WIDTH = 256
KINDS = ("square", "down", "gain")
RINGS = {
    "parts": {"square": 6, "down": 4, "gain": 2},
    "keep1": {"square": 5, "down": 4, "gain": 2},
    "keep2": {"square": 2, "down": 3, "gain": 2},
    "keepr": {"square": 3, "down": 3, "gain": 2},
    "keep3": {"square": 3, "down": 1, "gain": 1},
}
CROSS = {"square": 2, "down": 1, "gain": 1}
LEADS = ("0", "1", "2", "r", "z")
EARLY_OPS = (
    ("load", 2, "0"),
    ("add", 1, "0"),
    ("load", 4, "1"),
    ("add", 1, "1"),
    ("load", 3, "2"),
    ("add", 1, "2"),
    ("load", 2, "r"),
    ("add", 1, "r"),
    ("load", 2, "z"),
    ("add", 1, "z"),
)
LATE_OPS = (
    ("load", 2, "0"),
    ("add", 1, "0"),
    ("load", 4, "1"),
    ("add", 1, "1"),
    ("load", 3, "r"),
    ("add", 1, "r"),
    ("load", 3, "z"),
    ("add", 1, "z"),
    ("load", 2, "2"),
    ("add", 1, "2"),
)


def backward_pieces(width, ff_width):
    pieces = []
    for layer in (1, 0):
        for step, lo in enumerate(range(0, width, DOWN_WIDTH)):
            pieces.append(Piece("down", layer, 6, lo, lo + DOWN_WIDTH, step % 2 == 0, False))
        for lo in range(0, ff_width, width):
            hi = min(lo + width, ff_width)
            pieces.append(Piece("square", layer, 4, lo, hi, True, True))
            pieces.append(Piece("square", layer, 5, lo, hi, False, True))
        for item, x_first in ((3, True), (2, False), (1, True), (0, False)):
            pieces.append(Piece("square", layer, item, 0, width, x_first, item != 3))
        pieces.append(Piece("gain", layer, 7, 0, 128, True, False))
    seen = {kind: 0 for kind in KINDS}
    for index, piece in enumerate(pieces):
        piece.index = index
        piece.order = seen[piece.kind]
        seen[piece.kind] += 1
    return pieces, seen


def scatter_shapes(z_count):
    return {
        kind: {
            "0": (2, z_count, 2),
            "1": (z_count, 2),
            "2": (z_count,),
            "r": (2, CROSS[kind]),
            "z": (2, CROSS[kind]),
        }
        for kind in KINDS
    }


class Scatter:
    def __init__(self, z_count, pieces, groups, sums, semaphores):
        self.place = Place(z_count)
        self.pieces, self.groups, self.sums = pieces, groups, sums
        (
            self.send,
            self.recv,
            self.z_send,
            self.z_recv,
            self.relay_send,
            self.relay_recv,
            self.load_sem,
            self.out_sem,
        ) = semaphores
        self.sent, self.stored = set(), set()
        self.active = []
        self.now = 0
        self.busy = {}
        self.holders = {}

    def sides(self, piece):
        place = self.place
        return (place.x, place.y) if piece.x_first else (place.y, place.x)

    def body(self, piece):
        return (slice(None), pl.ds(0, piece.width))

    def across(self, piece):
        return ((slice(None),) if piece.late else (0,)) + self.body(piece)

    def hop(self, piece, stage):
        place, group, n = self.place, self.groups[piece.kind], piece.index
        first, second = self.sides(piece)
        c, body, every = place.c, self.body(piece), slice(None)
        first_mate, second_mate = place.x_mate(), place.y_mate()
        if not piece.x_first:
            first_mate, second_mate = second_mate, first_mate
        if stage == "0":
            source = group["parts"].at[(piece.slots["parts"], 1 - c, every, every, every) + body]
            target = group["recv0"].at[(piece.order, every, every, every) + body]
            mate = place.core_mate()
        elif stage == "1":
            source = group["parts"].at[(piece.slots["parts"], c, 1 - first, every, every) + body]
            target = group["recv1"].at[(piece.order, every, every) + body]
            mate = first_mate
        elif piece.late:
            source = group["keep3"].at[(piece.slots["keep3"], 1 - second) + body]
            target = group["recv2"].at[(piece.order, 0) + body]
            mate = second_mate
        else:
            source = group["keep1"].at[(piece.slots["keep1"], every, 1 - second) + body]
            target = group["recv2"].at[(piece.order, every) + body]
            mate = second_mate
        k = "012".index(stage)
        return remote(source, target, self.send.at[n, k], self.recv.at[n, k], mate)

    def z_source(self, piece, where):
        group = self.groups[piece.kind]
        name = "keep1" if piece.late else "keep2"
        lead = (slice(None),) if piece.late else ()
        return group[name].at[(piece.slots[name], where) + lead + self.body(piece)]

    def z_device(self, target):
        place = self.place
        return place.device(place.x, target, place.y, place.c)

    def z_neighbour(self):
        z = self.place.z
        return z + 1 - 2 * lax.rem(z, 2), z // 3

    def z_direct(self, piece):
        n = piece.index
        target, slot = self.z_neighbour()
        arrived = self.groups[piece.kind]["recvz"]
        return remote(
            self.z_source(piece, target),
            arrived.at[(piece.order, slot) + self.across(piece)],
            self.z_send.at[n, 0],
            self.z_recv.at[n, slot],
            self.z_device(target),
        )

    def z_sum(self, piece, index):
        place, group, n = self.place, self.groups[piece.kind], piece.index
        target = 2 * (2 - place.z) + index
        slot = place.z - 1 if index == 0 else 1
        return remote(
            group["keepr"].at[(piece.slots["keepr"], index) + self.across(piece)],
            group["recvz"].at[(piece.order, slot) + self.across(piece)],
            self.z_send.at[n, 1 + index],
            self.z_recv.at[n, slot],
            self.z_device(target),
        )

    def z_arrival(self, piece, slot):
        arrived = self.groups[piece.kind]["recvz"]
        ref = arrived.at[(piece.order, slot) + self.across(piece)]
        return remote(
            ref,
            ref,
            self.z_send.at[piece.index, 0],
            self.z_recv.at[piece.index, slot],
            self.z_device(self.z_neighbour()[0]),
        )

    def relay(self, piece):
        place, n = self.place, piece.index
        pair = pl.ds(2 - 2 * (place.z // 3), 2)
        arrived = self.groups[piece.kind]["recvr"]
        return remote(
            self.z_source(piece, pair),
            arrived.at[(piece.order, slice(None)) + self.across(piece)],
            self.relay_send.at[n],
            self.relay_recv.at[n],
            self.z_device(1 + place.z // 3),
        )

    def relay_arrival(self, piece):
        place, n = self.place, piece.index
        ref = self.groups[piece.kind]["recvr"].at[(piece.order, slice(None)) + self.across(piece)]
        return remote(
            ref, ref, self.relay_send.at[n], self.relay_recv.at[n], self.z_device(3 * (place.z - 1))
        )

    def window(self, piece, stage):
        every = slice(None)
        if stage == "0":
            return (every, every, every) + self.body(piece)
        if stage == "1":
            return (every, every) + self.body(piece)
        if stage == "2":
            return ((0,) if piece.late else (every,)) + self.body(piece)
        return (every,) + self.across(piece)

    def load(self, piece, stage):
        group, where = self.groups[piece.kind], self.window(piece, stage)
        return pltpu.make_async_copy(
            group["recv" + stage].at[(piece.order,) + where],
            group["temp" + stage].at[where],
            self.load_sem.at[KINDS.index(piece.kind), LEADS.index(stage)],
        )

    def out_copy(self, piece):
        group = self.groups[piece.kind]
        return pltpu.make_async_copy(
            group["stage"].at[self.body(piece)],
            self.sums[piece.item].at[piece.layer, :, pl.ds(piece.lo, piece.width)],
            self.out_sem.at[piece.index],
        )

    def on_middle(self, fn):
        pl.when(self.place.is_middle())(fn)

    def on_end(self, fn):
        pl.when(jnp.logical_not(self.place.is_middle()))(fn)

    def settle(self, piece, stage):
        if (piece.index, stage) in self.sent:
            return
        self.sent.add((piece.index, stage))
        if stage in "012":
            self.hop(piece, stage).wait_send()
        elif stage == "d":
            self.z_direct(piece).wait_send()
            self.on_end(lambda: self.relay(piece).wait_send())
        else:

            def sums():
                for index in range(2):
                    self.z_sum(piece, index).wait_send()

            self.on_middle(sums)

    def holder(self, piece, name):
        count = RINGS[name][piece.kind]
        used = self.holders.setdefault((piece.kind, name), [])
        return len(used) % count, used[-count] if len(used) >= count else None

    def can_claim(self, piece, name):
        other = self.holder(piece, name)[1]
        if other is None:
            return True
        last = {"parts": ("add", "1"), "keepr": ("add", "r"), "keep3": ("add", "2"), "keep2": ("add", "z")}
        if name == "keep1":
            need = ("add", "z") if other.late else ("add", "2")
        else:
            need = last[name]
        names = [(op[0], op[2]) for op in other.ops]
        return other.done > names.index(need)

    def claim(self, piece, name):
        slot, other = self.holder(piece, name)
        if other is not None:
            for stage in {
                "parts": "01",
                "keep1": "d" if other.late else "2",
                "keep2": "d",
                "keepr": "s",
                "keep3": "2",
            }[name]:
                self.settle(other, stage)
        self.holders[(piece.kind, name)].append(piece)
        piece.slots[name] = slot
        return slot

    def open(self, piece):
        while not self.can_claim(piece, "parts"):
            self.tick()
        return self.claim(piece, "parts")

    def launch(self, piece):
        self.hop(piece, "0").start()
        piece.moved = self.now
        self.active.append(piece)

    def claims(self, piece, stage):
        if stage == "1":
            return "keep1"
        if stage == "2" and not piece.late:
            return "keep2"
        if stage == "r":
            return "keepr"
        if stage == "z" and piece.late:
            return "keep3"
        return None

    def add(self, piece, stage):
        group = self.groups[piece.kind]
        place, columns = self.place, pl.ds(0, piece.width)
        body = self.body(piece)
        first, second = self.sides(piece)
        c, slots, every = place.c, piece.slots, slice(None)
        parts, keep1, keep2 = group["parts"], group["keep1"], group["keep2"]
        keepr, keep3 = group["keepr"], group["keep3"]
        temp = group["temp" + stage]
        last = piece.ops[-1][2] == stage
        if last:
            before = [p for p in self.pieces if p.kind == piece.kind and p.order == piece.order - 1]
            if before and before[0].index not in self.stored:
                self.stored.add(before[0].index)
                self.out_copy(before[0]).wait()
            if piece.late:
                value = keep3[(slots["keep3"], second) + body].astype(jnp.float32)
                value = value + temp[(0,) + body].astype(jnp.float32)
            else:
                value = keep2[(slots["keep2"], place.z) + body].astype(jnp.float32)
                for slot in range(2):
                    value = value + temp[(slot, 0) + body].astype(jnp.float32)
            group["stage"][:, columns] = value
            self.out_copy(piece).start()
            return
        if stage in "01":

            @pl.loop(0, place.z_count)
            def _(k):
                if stage == "0":
                    for a in range(2):
                        where = (a, k, every) + body
                        at = (slots["parts"], c) + where
                        parts[at] = parts[at] + temp[where]
                else:
                    where = (k, every) + body
                    keep1[(slots["keep1"],) + where] = (
                        parts[(slots["parts"], c, first) + where] + temp[where]
                    )

        if stage == "0":
            self.hop(piece, "1").start()
        if stage == "1" and not piece.late:
            self.hop(piece, "2").start()
        if stage == "2":

            @pl.loop(0, place.z_count)
            def _(k):
                keep2[(slots["keep2"], k) + body] = (
                    keep1[(slots["keep1"], k, second) + body] + temp[(k,) + body]
                )

        if (stage == "1" and piece.late) or stage == "2":
            self.z_direct(piece).start()
            self.on_end(lambda: self.relay(piece).start())
        if stage == "r":
            own = keep1 if piece.late else keep2
            name = "keep1" if piece.late else "keep2"
            lead = (every,) if piece.late else ()
            for index in range(2):
                target = 2 * (2 - place.z) + index
                value = own[(slots[name], target) + lead + body]
                where = (index,) + self.across(piece)
                keepr[(slots["keepr"],) + where] = value + temp[where]
                self.z_sum(piece, index).start()
        if stage == "z":
            value = keep1[(slots["keep1"], place.z, every) + body].astype(jnp.float32)
            for slot in range(2):
                value = value + temp[(slot, every) + body].astype(jnp.float32)
            keep3[(slots["keep3"], every) + body] = value.astype(keep3.dtype)
            self.hop(piece, "2").start()

    def perform(self, piece):
        name, unused, stage = piece.ops[piece.done]
        if name == "load":
            self.busy[(piece.kind, stage)] = True
            if stage in "012":
                self.hop(piece, stage).wait_recv()
                self.load(piece, stage).start()
            elif stage == "r":

                def fetch():
                    self.relay_arrival(piece).wait_recv()
                    self.load(piece, stage).start()

                self.on_middle(fetch)
            else:
                for slot in range(2):
                    self.z_arrival(piece, slot).wait_recv()
                self.load(piece, stage).start()
        else:
            self.busy[(piece.kind, stage)] = False
            ring = self.claims(piece, stage)
            if ring:
                self.claim(piece, ring)

            def finish():
                self.load(piece, stage).wait()
                self.add(piece, stage)

            if stage == "r":
                self.on_middle(finish)
            else:
                finish()
        piece.done += 1
        piece.moved = self.now

    def tick(self):
        self.now += 1
        for piece in list(self.active):
            name, lag, stage = piece.ops[piece.done]
            if self.now < piece.moved + lag:
                continue
            if name == "load" and self.busy.get((piece.kind, stage)):
                continue
            ring = self.claims(piece, stage) if name == "add" else None
            if ring and not self.can_claim(piece, ring):
                continue
            self.perform(piece)
            if piece.done == len(piece.ops):
                self.active.remove(piece)

    def finish(self):
        while self.active:
            self.tick()
        for piece in self.pieces:
            for stage in "012ds":
                self.settle(piece, stage)
            if piece.index not in self.stored:
                self.out_copy(piece).wait()


def norm_rows_backward(source, gain_row, grad_normed, grad, low, gain_sum):
    gain_sum[...] = jnp.zeros_like(gain_sum)
    width = source.shape[1]

    @pl.loop(0, source.shape[0] // 64)
    def _(step):
        rows = pl.ds(pl.multiple_of(step * 64, 64), 64)
        value = source[rows, :]
        inverse = lax.rsqrt(jnp.mean(value * value, axis=1, keepdims=True) + EPSILON)
        unit = value * inverse
        normed = grad_normed[rows, :]
        gain_sum[...] += jnp.sum((normed * unit).reshape(8, 8, width), axis=0)
        grad_unit = normed * gain_row
        inner = jnp.mean(grad_unit * unit, axis=1, keepdims=True)
        total = grad[rows, :] + inverse * (grad_unit - unit * inner)
        grad[rows, :] = total
        low[rows, :] = total.astype(low.dtype)


def attend_pairs_backward(
    start, stop, layer, query, key, value, mask, grad_context, norms, carried, cosine, sine
):
    rows = mask.shape[0]
    block = rows // 2

    @pl.loop(start, stop)
    def _(pair):
        lanes = pl.ds(pl.multiple_of(pair * 128, 128), 128)
        key_sum = [None, None]
        value_sum = [None, None]
        query_grads = []
        for q_index in range(2):
            q_rows = pl.ds(q_index * block, block)
            keys = (q_index + 1) * block
            q_block = query(q_rows, lanes)
            c_block = grad_context[q_rows, lanes]
            k_block = key(pl.ds(0, keys), lanes)
            v_block = value(pl.ds(0, keys), lanes)
            lane = lax.broadcasted_iota(jnp.int32, (block, 128), 1)
            key_lane = lax.broadcasted_iota(jnp.int32, (keys, 128), 1)
            allowed = mask[q_rows, 0:keys].astype(jnp.float32) > 0
            grad_q = None
            grad_k = None
            grad_v = None
            for head in range(2):
                own = (lane < 64) if head == 0 else (lane >= 64)
                key_own = (key_lane < 64) if head == 0 else (key_lane >= 64)
                q_own = jnp.where(own, q_block, jnp.zeros_like(q_block))
                c_own = jnp.where(own, c_block, jnp.zeros_like(c_block))
                k_own = jnp.where(key_own, k_block, jnp.zeros_like(k_block))
                norm = jnp.sum(
                    jnp.where(lane == 2 * pair + head, norms[q_rows, :], 0.0),
                    axis=1,
                    keepdims=True,
                )
                scores = times_transposed(q_own, k_block)
                prob = jnp.where(allowed, jnp.exp(scores - norm), 0.0)
                grad_prob = times_transposed(c_own, v_block)
                inner = jnp.sum(prob * grad_prob, axis=1, keepdims=True)
                grad_scores = (prob * (grad_prob - inner)).astype(jnp.bfloat16)
                prob_low = prob.astype(jnp.bfloat16)
                terms = (
                    matmul(grad_scores, k_own),
                    inner_rows(q_own, grad_scores),
                    inner_rows(c_own, prob_low),
                )
                if head == 0:
                    grad_q, grad_k, grad_v = terms
                else:
                    grad_q, grad_k, grad_v = (
                        grad_q + terms[0],
                        grad_k + terms[1],
                        grad_v + terms[2],
                    )
            query_grads.append(grad_q * HD ** (-0.5))
            for k_index in range(q_index + 1):
                part = slice(k_index * block, (k_index + 1) * block)
                for sums, term in ((key_sum, grad_k), (value_sum, grad_v)):
                    piece = term[:, part]
                    sums[k_index] = piece if sums[k_index] is None else sums[k_index] + piece
        for index in range(2):
            where = pl.ds(index * block, block)
            cos_block, sin_block = cosine[where, :], -sine[where, :]
            grad_q = turn(query_grads[index], cos_block, sin_block)
            query(where, lanes, grad_q.astype(jnp.bfloat16))
            grad_k = turn(key_sum[index].T, cos_block, sin_block)
            key(where, lanes, grad_k.astype(jnp.bfloat16))
            grad_v = value_sum[index].T
            if layer == 1:
                low = (0.5 * grad_v).astype(jnp.bfloat16)
            else:
                low = (grad_v + carried(where, lanes).astype(jnp.float32)).astype(jnp.bfloat16)
            value(where, lanes, low)


def columns_of(ref, base):
    def access(rows, lanes, value=None):
        inner = pl.ds(pl.multiple_of(lanes.start + base, 128), lanes.size)
        if value is None:
            return ref[rows, inner]
        ref[rows, inner] = value

    return access


def backward_kernel(z_count, pieces, gain_rows, *refs):
    refs = list(refs)

    def take(count):
        taken = refs[:count]
        del refs[:count]
        return taken

    gathered = take(14)
    kept = [dict(zip(KEPT, take(len(KEPT)))) for unused in (0, 1)]
    (cotangent,) = take(1)
    gains, mask, cosine, sine, live = take(5)
    sums = take(8)
    grad_tokens, spill = take(2)
    groups = {kind: {} for kind in KINDS}
    for kind in KINDS:
        for stage in LEADS:
            (groups[kind]["recv" + stage],) = take(1)
    for kind in KINDS:
        for name in list(RINGS) + ["temp" + stage for stage in LEADS] + ["stage"]:
            (groups[kind][name],) = take(1)
    grad, xbuf, normed, low, gbuf, ubuf, hbuf, tbuf, gctx, lse, rowbuf, gain_sum = take(12)
    load_sem, row_sem, stream_sem = take(3)
    scatter = Scatter(z_count, pieces, groups, sums, take(8))
    width, ff_width = grad.shape[1], gbuf.shape[1]
    queue = list(pieces)
    blocks = -(-ff_width // width)
    names = KEPT + ("cot", "out", "carried")

    def load_of(layer, name):
        every = slice(None)
        targets = {
            "ht": hbuf,
            "g": gbuf,
            "u": ubuf,
            "n2t": tbuf,
            "mid": xbuf,
            "ctxt": tbuf,
            "lse": lse,
            "n1t": tbuf,
            "q": gbuf.at[every, pl.ds(0, width)],
            "k": gbuf.at[every, pl.ds(width, width)],
            "v": ubuf.at[every, pl.ds(0, width)],
            "hid": xbuf,
            "carried": ubuf.at[every, pl.ds(width, width)],
        }
        source = spill if name == "carried" else kept[layer][name]
        return pltpu.make_async_copy(source, targets[name], load_sem.at[names.index(name)])

    def start(layer, *which):
        for name in which:
            load_of(layer, name).start()

    def wait(layer, *which):
        for name in which:
            load_of(layer, name).wait()

    def flat(item):
        ref = gathered[item]
        return ref.reshape(z_count * 8 * ref.shape[4], ref.shape[5])

    def down_copies(layer):
        ref = gathered[7 * layer + 6]
        step = ref.shape[4]
        places = itertools.product(range(2), range(z_count), range(2), range(2))
        return [
            pltpu.make_async_copy(
                ref.at[where], rowbuf.at[pl.ds(index * step, step)], row_sem.at[index]
            )
            for index, where in enumerate(places)
        ]

    def square_copy(layer, item, at):
        return pltpu.make_async_copy(
            flat(7 * layer + item), rowbuf.at[pl.ds(at * width, width)], row_sem.at[at]
        )

    def stream_copy(layer, index):
        row, column, side = index // (2 * blocks), index % (2 * blocks) // 2, index % 2
        lo = column * width
        size = min(width, ff_width - lo)
        slot = index % 8
        target = rowbuf.at[pl.ds(width + slot * 256, 256), pl.ds(0, size)]
        source = flat(7 * layer + 4 + side).at[pl.ds(row * 256, 256), pl.ds(lo, size)]
        return pltpu.make_async_copy(source, target, stream_sem.at[slot])

    def start_all(copies):
        for copy in copies:
            copy.start()

    def wait_all(copies):
        for copy in copies:
            copy.wait()

    def produce(left, right, base):
        piece = queue.pop(0)
        slot = scatter.open(piece)
        parts = groups[piece.kind]["parts"]
        row_count = parts.shape[5]
        span = z_count if piece.kind == "square" else 1
        depth = 4 * row_count * span

        def store(x_index, z_start, columns, block):
            block = block.reshape(span, 2, 2, row_count, 256).astype(jnp.bfloat16)
            zs = pl.ds(z_start, span)
            for y_index in range(2):
                for core in range(2):
                    a, b = (x_index, y_index) if piece.x_first else (y_index, x_index)
                    parts[slot, core, a, zs, b, :, columns] = block[:, y_index, core]

        @tiles(0, piece.width, 256)
        def _(columns):
            inner = pl.ds(pl.multiple_of(columns.start + piece.lo + base, 256), 256)
            for x_index in range(2):
                for z_start in range(0, z_count, span):
                    first = (x_index * z_count + z_start) * 4 * row_count
                    block = matmul(left[first : first + depth, :], right[:, inner])
                    store(x_index, z_start, columns, block)

        scatter.launch(piece)

    def produce_gains():
        piece = queue.pop(0)
        slot = scatter.open(piece)
        parts = groups["gain"]["parts"]
        row_count = z_count * 64
        row = lax.broadcasted_iota(jnp.int32, (row_count, width), 0)
        column = lax.broadcasted_iota(jnp.int32, (row_count, width), 1)
        own = row == (column // gain_rows) * 8
        source = lax.broadcasted_iota(jnp.int32, (width, 128), 0)
        lane = lax.broadcasted_iota(jnp.int32, (width, 128), 1)
        total = jnp.zeros((row_count, 128), jnp.float32)
        for index in range(2):
            pick = (lane == index * gain_rows + source % gain_rows).astype(jnp.bfloat16)
            line = jnp.sum(gain_sum[index], axis=0, keepdims=True)
            spread = jnp.where(own, jnp.broadcast_to(line, (row_count, width)), 0.0)
            high = spread.astype(jnp.bfloat16)
            rest = (spread - high.astype(jnp.float32)).astype(jnp.bfloat16)
            total = total + matmul(high, pick) + matmul(rest, pick)
        total = total.reshape(2, z_count, 2, 2, 8, 128)
        for x_index in range(2):
            for y_index in range(2):
                for core in range(2):
                    parts[slot, core, x_index, :, y_index] = total[x_index, :, y_index, core]
        scatter.launch(piece)

    def layer_steps(layer):
        if layer == 1:
            start_cot = pltpu.make_async_copy(cotangent, low, load_sem.at[names.index("cot")])
            start_cot.start()
            start(layer, "ht", "g", "u", "n2t", "mid", "lse")
            start_all(down_copies(layer))
            start_cot.wait()

            @pl.loop(0, grad.shape[0] // 64)
            def _(step):
                rows = pl.ds(pl.multiple_of(step * 64, 64), 64)
                value = low[rows, :].astype(jnp.float32) * live[rows, 0:1]
                grad[rows, :] = value
                low[rows, :] = value.astype(jnp.bfloat16)

        wait(layer, "ht")
        for unused in range(width // DOWN_WIDTH):
            produce(hbuf, low, 0)
            yield
        if layer == 1:
            start(0, "ht")
        wait(layer, "g", "u")
        wait_all(down_copies(layer))
        tile_count = ff_width // 256
        for lo in range(0, tile_count, 4):

            @tiles(lo * 256, min(lo + 4, tile_count) * 256, 256)
            def _(columns):
                into = times_transposed(low[...], rowbuf[columns, :])
                gate = gbuf[:, columns].astype(jnp.float32)
                up = ubuf[:, columns].astype(jnp.float32)
                sigma = jax.nn.sigmoid(gate)
                slope = sigma * (1.0 + gate * (1.0 - sigma))
                gbuf[:, columns] = (into * up * slope).astype(jnp.bfloat16)
                ubuf[:, columns] = (into * gate * sigma).astype(jnp.bfloat16)

            yield
        square_copy(layer, 3, 0).start()
        start_all([stream_copy(layer, index) for index in range(8)])
        wait(layer, "n2t")
        for lo in range(0, ff_width, width):
            produce(tbuf, gbuf, 0)
            yield
            produce(tbuf, ubuf, 0)
            yield
        start(layer, "ctxt")
        count = 2 * blocks * (width // 256)
        total = None
        for index in range(count):
            stream_copy(layer, index).wait()
            lo = index % (2 * blocks) // 2 * width
            size = min(width, ff_width - lo)
            left = (gbuf, ubuf)[index % 2][:, lo : lo + size]
            at = width + index % 8 * 256
            block = times_transposed(left, rowbuf[at : at + 256, 0:size])
            total = block if total is None else total + block
            if index + 8 < count:
                stream_copy(layer, index + 8).start()
            if index % (2 * blocks) == 2 * blocks - 1:
                at = index // (2 * blocks) * 256
                normed[:, at : at + 256] = total
                total = None
                yield
        start_all([square_copy(layer, 0, 1), square_copy(layer, 1, 2)])
        start(layer, "q", "k", "v")
        if layer == 0:
            start(layer, "carried")
        wait(layer, "mid")
        norm_rows_backward(
            xbuf, gains[layer + 2 : layer + 3, :], normed, grad, low, gain_sum.at[1]
        )
        start(layer, "hid")
        yield
        wait(layer, "ctxt")
        produce(tbuf, low, 0)
        start(layer, "n1t")
        yield
        square_copy(layer, 3, 0).wait()

        @tiles(0, width, 256)
        def _(columns):
            gctx[:, columns] = times_transposed(low[...], rowbuf[columns, :]).astype(jnp.bfloat16)

        square_copy(layer, 2, 0).start()
        wait(layer, "q", "k", "v", "lse")
        if layer == 0:
            wait(layer, "carried")
        yield
        for pair in range(0, H // 2, 2):
            attend_pairs_backward(
                pair,
                pair + 2,
                layer,
                columns_of(gbuf, 0),
                columns_of(gbuf, width),
                columns_of(ubuf, 0),
                mask,
                gctx,
                lse,
                columns_of(ubuf, width),
                cosine,
                sine,
            )
            yield
        if layer == 1:
            spilled = pltpu.make_async_copy(
                ubuf.at[:, pl.ds(0, width)], spill, load_sem.at[names.index("carried")]
            )
            spilled.start()
            start(0, "lse")
        wait(layer, "n1t")
        produce(tbuf, ubuf, 0)
        yield
        produce(tbuf, gbuf, width)
        yield
        produce(tbuf, gbuf, 0)
        yield
        if layer == 1:
            start(0, "n2t")
        for at in (1, 2, 0):
            square_copy(layer, (2, 0, 1)[at], at).wait()

        @tiles(0, width, 256)
        def _(columns):
            def block(at):
                return rowbuf[pl.ds(pl.multiple_of(columns.start + at * width, 256), 256), :]

            total = times_transposed(gbuf[:, 0:width], block(1))
            total = total + times_transposed(gbuf[:, width : 2 * width], block(2))
            normed[:, columns] = total + times_transposed(ubuf[:, 0:width], block(0))

        if layer == 1:
            spilled.wait()
            start(0, "g", "u")
            start_all(down_copies(0))
        yield
        wait(layer, "hid")
        norm_rows_backward(xbuf, gains[layer : layer + 1, :], normed, grad, low, gain_sum.at[0])
        if layer == 1:
            start(0, "mid")
        produce_gains()
        yield

    greet(scatter.place)
    for layer in (1, 0):
        for unused in layer_steps(layer):
            scatter.tick()
    last = pltpu.make_async_copy(low, grad_tokens, load_sem.at[names.index("out")])
    last.start()
    scatter.finish()
    last.wait()


def backward(z_count, gathered, kept, cotangent, gains, mask, cosine, sine, live):
    rows, width = cotangent.shape
    ff_width = gathered[4].shape[5]
    pieces, counts = backward_pieces(width, ff_width)
    low, wide = jnp.bfloat16, jnp.float32
    square_rows, down_rows = gathered[0].shape[4], gathered[6].shape[4]
    gain_rows = square_rows
    shapes = {
        "square": (square_rows, width, low),
        "down": (down_rows, DOWN_WIDTH, low),
        "gain": (8, 128, wide),
    }
    any_spec = pl.BlockSpec(memory_space=pl.ANY)
    vmem_spec = pl.BlockSpec(memory_space=pltpu.VMEM)
    received, scratch = [], []
    leads = scatter_shapes(z_count)
    for kind in KINDS:
        r, w, dtype = shapes[kind]
        for stage in LEADS:
            lead = (counts[kind],) + leads[kind][stage]
            received.append(jax.ShapeDtypeStruct(lead + (r, w), dtype))
        inner = {
            "parts": (2, 2, z_count, 2),
            "keep1": (z_count, 2),
            "keep2": (z_count,),
            "keepr": (2, CROSS[kind]),
            "keep3": (CROSS[kind],),
        }
        for name in RINGS:
            scratch.append(pltpu.VMEM((RINGS[name][kind],) + inner[name] + (r, w), dtype))
        for stage in LEADS:
            scratch.append(pltpu.VMEM(leads[kind][stage] + (r, w), dtype))
        scratch.append(pltpu.VMEM((r, w), wide))
    scratch += [
        pltpu.VMEM((rows, width), wide),
        pltpu.VMEM((rows, width), wide),
        pltpu.VMEM((rows, width), wide),
        pltpu.VMEM((rows, width), low),
        pltpu.VMEM((rows, ff_width), low),
        pltpu.VMEM((rows, ff_width), low),
        pltpu.VMEM((ff_width, rows), low),
        pltpu.VMEM((width, rows), low),
        pltpu.VMEM((rows, width), low),
        pltpu.VMEM((rows, 128), wide),
        pltpu.VMEM((max(ff_width, 3 * width), width), low),
        pltpu.VMEM((2, 8, width), wide),
        pltpu.SemaphoreType.DMA((len(KEPT) + 3,)),
        pltpu.SemaphoreType.DMA((z_count * 8,)),
        pltpu.SemaphoreType.DMA((8,)),
    ]
    total = len(pieces)
    scratch += [
        pltpu.SemaphoreType.DMA((total, 3)),
        pltpu.SemaphoreType.DMA((total, 3)),
        pltpu.SemaphoreType.DMA((total, 3)),
        pltpu.SemaphoreType.DMA((total, 2)),
        pltpu.SemaphoreType.DMA((total,)),
        pltpu.SemaphoreType.DMA((total,)),
        pltpu.SemaphoreType.DMA((len(KINDS), len(LEADS))),
        pltpu.SemaphoreType.DMA((total,)),
    ]
    sums = [jax.ShapeDtypeStruct((2,) + g.shape[4:], wide) for g in gathered[:7]]
    sums.append(jax.ShapeDtypeStruct((2, 8, 128), wide))
    results = pl.pallas_call(
        functools.partial(backward_kernel, z_count, pieces, gain_rows),
        name="backward_scatter",
        out_shape=tuple(sums) + (jax.ShapeDtypeStruct((rows, width), low),) * 2 + tuple(received),
        in_specs=[any_spec] * (14 + 2 * len(KEPT) + 1) + [vmem_spec] * 5,
        out_specs=[any_spec] * (10 + len(received)),
        scratch_shapes=scratch,
        compiler_params=pltpu.CompilerParams(
            collective_id=3, has_side_effects=True, vmem_limit_bytes=VMEM_BYTES
        ),
    )(
        *gathered[:14],
        *[kept[layer][name] for layer in (0, 1) for name in KEPT],
        cotangent,
        gains,
        mask,
        cosine,
        sine,
        live,
    )
    return results[:8], results[8]


def ff_split(ff_width):
    return (ff_width // 2 + 255) // 256 * 256


def gather_chunks(base, width, ff_width):
    half, middle = ff_split(ff_width), width // 2
    chunks = []
    for left, right, lo, hi in (
        (0, 1, 0, width),
        (2, 3, 0, width),
        (4, 5, 0, half),
        (4, 5, half, ff_width),
    ):
        cut = lo + (hi - lo) // 256 * 128
        for start, stop in ((lo, cut), (cut, hi)):
            chunks.append([(base + left, start, stop), (base + right, start, stop)])
    for lo in (0, middle):
        cut = lo + middle // 2
        chunks.append([(base + 6, lo, cut), (base + 6, cut, lo + middle)])
    return chunks


def gather_orders(chunks):
    orders = (("xzy", "yzx"), ("zxy", "zyx"), ("xzy", "yzx"))
    return [
        [piece + (orders[index % 3][side],) for side, piece in enumerate(chunk)]
        for index, chunk in enumerate(chunks)
    ]


def layer_chunks(base, width, ff_width):
    half = ff_split(ff_width)
    cut = (width // 2) // 128 * 128
    return [
        [(base, 0, width, True), (base + 1, 0, width, False)],
        [(base + 2, 0, width, True), (base + 3, 0, width, False)],
        [(base + 4, 0, half, True), (base + 5, 0, half, False)],
        [(base + 4, half, ff_width, True), (base + 5, half, ff_width, False)],
        [(base + 6, 0, cut, True), (base + 6, cut, width, False)],
    ]


def body(
    z_count,
    tokens,
    doc_ids,
    live_mask,
    w_query,
    w_key,
    w_value,
    w_out,
    w_gate,
    w_up,
    w_down,
    gain_attn,
    gain_ffn,
    cotangent,
):
    stacked_weights = (w_query, w_key, w_value, w_out, w_gate, w_up, w_down)
    width, ff_width = w_query.shape[2], w_gate.shape[2]
    gain_rows = gain_attn.shape[1]
    chunks = gather_chunks(0, width, ff_width) + gather_chunks(7, width, ff_width)
    chunks = gather_orders(chunks)
    chunks[0] = [(14, 0, 128, "zxy")] + chunks[0]
    if z_count == 4 and gain_rows % 16 == 0 and w_down.shape[1] % 8 == 0:
        gathered, kept, tables, output = forward(
            z_count,
            stacked_weights,
            chunks,
            ff_split(ff_width),
            tokens,
            doc_ids[None, :],
            live_mask[None, :],
            gain_attn,
            gain_ffn,
        )
        sums, grad_tokens = backward(z_count, gathered, kept, cotangent, *tables)
        gain_sums = [sums[7][:, 0, k * gain_rows : (k + 1) * gain_rows] for k in (0, 1)]
        return (output, grad_tokens) + tuple(sums[:7]) + tuple(gain_sums)
    position, allowed = sequence_layout(doc_ids, live_mask)
    cosine, sine_table = rope_tables(position)
    gains = jnp.concatenate([gain_attn, gain_ffn], axis=0).astype(jnp.float32).reshape(-1)
    gain_pad = -gains.shape[0] % 1024
    gain_block = jnp.pad(gains, (0, gain_pad)).reshape(-1, 128)
    shards = [weight[layer] for layer in (0, 1) for weight in stacked_weights] + [gain_block]
    gathered = gather_weights(z_count, shards, chunks)
    device_count = z_count * 8
    full_gains = gathered[14].reshape(device_count, -1)[:, : 4 * gain_rows]
    full_gains = full_gains.reshape(device_count, 4, gain_rows).transpose(1, 0, 2).reshape(4, -1)
    full_gains = full_gains.astype(jnp.bfloat16)

    def layer_params(layer):
        matrices = gathered[7 * layer : 7 * layer + 7]
        whole = tuple(matrix.reshape(-1, matrix.shape[-1]) for matrix in matrices)
        return whole + (full_gains[layer], full_gains[2 + layer])

    def reduce_layer(grads):
        low = [grad.astype(jnp.bfloat16) for grad in grads[:7]]
        split = [grad.reshape(2, z_count, 2, 2, -1, grad.shape[-1]) for grad in low]
        gain_grads = jnp.stack(grads[7:9]).reshape(2, device_count, gain_rows)
        gain_grads = gain_grads.transpose(1, 0, 2).reshape(device_count, 2 * gain_rows)
        pad = -2 * gain_rows % 1024
        gain_grads = jnp.pad(gain_grads, ((0, 0), (0, pad)))
        split.append(gain_grads.reshape(2, z_count, 2, 2, -1, 128))
        order = layer_chunks(0, width, ff_width)[::-1]
        order[-1] = order[-1] + [(7, 0, 128, True)]
        sums = scatter_grads(z_count, split, order)
        gain_sums = sums[7].reshape(-1)[: 2 * gain_rows].reshape(2, gain_rows)
        return tuple(sums[:7]) + (gain_sums[0], gain_sums[1])

    params_one, params_two = layer_params(0), layer_params(1)
    middle_rows, values_first, saved_one = layer_forward(
        tokens.astype(jnp.float32), params_one, None, allowed, cosine, sine_table
    )
    result, unused_values, saved_two = layer_forward(
        middle_rows, params_two, values_first, allowed, cosine, sine_table
    )
    live_rows = live_mask.astype(jnp.float32)[:, None]
    output = (live_rows * result).astype(jnp.bfloat16)
    grad_result = cotangent.astype(jnp.float32) * live_rows
    grad_middle_rows, grads_two, carried = layer_backward(
        grad_result, params_two, saved_two, None, True, allowed, cosine, sine_table
    )
    shards_two = reduce_layer(grads_two)
    grad_hidden, grads_one, unused_carry = layer_backward(
        grad_middle_rows, params_one, saved_one, carried, False, allowed, cosine, sine_table
    )
    shards_one = reduce_layer(grads_one)
    stacked = tuple(jnp.stack([one, two]) for one, two in zip(shards_one, shards_two))
    return (output, grad_hidden.astype(jnp.bfloat16)) + stacked


def solution(mesh):
    in_specs = (
        P(("dp", "fsdp"), None),
        P(("dp", "fsdp")),
        P(("dp", "fsdp")),
        P(None, ("dp", "fsdp"), None),
        P(None, ("dp", "fsdp"), None),
        P(None, ("dp", "fsdp"), None),
        P(None, ("dp", "fsdp"), None),
        P(None, ("dp", "fsdp"), None),
        P(None, ("dp", "fsdp"), None),
        P(None, ("dp", "fsdp"), None),
        P(None, ("dp", "fsdp")),
        P(None, ("dp", "fsdp")),
        P(("dp", "fsdp"), None),
    )
    out_specs = (
        P(("dp", "fsdp"), None),
        P(("dp", "fsdp"), None),
        P(None, ("dp", "fsdp"), None),
        P(None, ("dp", "fsdp"), None),
        P(None, ("dp", "fsdp"), None),
        P(None, ("dp", "fsdp"), None),
        P(None, ("dp", "fsdp"), None),
        P(None, ("dp", "fsdp"), None),
        P(None, ("dp", "fsdp"), None),
        P(None, ("dp", "fsdp")),
        P(None, ("dp", "fsdp")),
    )
    run = functools.partial(body, mesh.shape["fsdp"] // 4)
    return jax.shard_map(run, mesh=mesh, in_specs=in_specs, out_specs=out_specs, check_vma=False)
```
